32 devices in a mesh: groups: 2 (over y), cand: 4 (over z), mp: 4 (over x, core).
Axes of the slice: x: 2, y: 2, z: 4, core: 2. Of those that a mesh axis runs over, the one named last changes fastest.
Arguments:
- user_feats: bfloat16 [8, 4096], P(('groups', 'cand')), parts along dimension 0, may hold values from -6 to 6
- user_slot: int32 [2], P('groups'), parts along dimension 0, may hold values from 0 to 3, as said below
- cand_pool: bfloat16 [512, 4096], P('groups'), parts along dimension 0, may hold values from -6 to 6
- cand_ids: int32 [2, 64], P('groups'), parts along dimension 0, may hold values from 0 to 255
- first_weight: bfloat16 [8192, 8192], P('mp', 'cand'), may hold values from -0.0625 to 0.0625
- first_bias: float32 [8192], P('cand'), may hold values from -5 to 5
- second_weight: bfloat16 [8192, 8192], P('cand', 'mp'), may hold values from -0.0625 to 0.0625
- second_bias: float32 [8192], P('mp'), may hold values from -5 to 5
- third_weight: bfloat16 [8192, 8192], P('mp', 'cand'), may hold values from -0.0625 to 0.0625
- third_bias: float32 [8192], P('cand'), may hold values from -5 to 5
- score_weight: bfloat16 [8192], P('cand'), may hold values from -0.0625 to 0.0625
Outputs:
- crossed: bfloat16 [128, 8192], P(('groups', 'mp'), 'cand'), parts along dimension 0
- logits: float32 [128], P(('groups', 'mp')), parts along dimension 0
The draws below stay inside these ranges and needn't reach their ends.
There are 2 independent parts, one for each index of `groups`. The reference program is written for one: setup_inputs(seed, part) draws one part's arguments, and reference() takes and returns one part's arrays. A program takes and returns all parts, laid end to end along the dimension named above; an argument that names none is the same for every part. Nothing has to cross between parts.
Inputs may be any that keep to these rules, and one draw needn't show every extreme that they name: `user_slot`: the users' slots are distinct.
All inputs are finite; a program needn't handle non-finite values.
Results may differ from the reference program's by a relative error of at most 0.022.
Values may be sent and summed in bfloat16 or wider, within the bound.
No kernel may reach another device: no remote copies, remote signals or barrier semaphores. Data moves between devices by JAX's collectives and lax.ppermute only.
A program may use at most 64 MiB of HBM per device.

```python
import jax
import jax.numpy as jnp
from jax import lax

DH = 4096
D = 8192
POOL = 256
CANDS = 64
USERS = 1
SLOTS = 4
ROWS = 64
N_CAND = 4


def draw_user_slot(key, part):
    pairs = jax.random.permutation(jax.random.fold_in(key, 11), SLOTS // 2)[:USERS].astype(jnp.int32)
    bits = jax.random.randint(jax.random.fold_in(key, 12), (USERS,), 0, 2).astype(jnp.int32)
    first_bit = (jnp.asarray(part).astype(jnp.int32) % 2).astype(jnp.int32)
    bits = bits.at[0].set(first_bit)
    return (2 * pairs + bits).astype(jnp.int32)


def with_ends(drawn, key, low, largest):
    longest = drawn.shape.index(max(drawn.shape))
    spots = []
    for shift in (0, 1):
        where = [jax.random.randint(jax.random.fold_in(key, axis), (), 0, length) for axis, length in enumerate(drawn.shape)]
        where[longest] = (where[longest] + shift) % drawn.shape[longest]
        spots.append(tuple(where))
    return drawn.at[spots[0]].set(low).at[spots[1]].set(largest)


def block_scale(rng, dims, split, smallest, largest):
    def one(dim, blocks):
        steps = jax.random.uniform(jax.random.fold_in(jax.random.fold_in(rng, 6), dim), (blocks,), jnp.float32, smallest / len(split), largest / len(split))
        return jnp.repeat(jnp.exp(steps), dims[dim] // blocks).reshape((-1,) + (1,) * (len(dims) - dim - 1))

    level = one(*split[0])
    for cut in split[1:]:
        level = level * one(*cut)
    return level


def gaussian(key, shape, scale, limit, pieces=(), held_as=jnp.bfloat16):
    array = scale * jax.random.normal(key, shape, jnp.float32)
    if pieces:
        array = array * block_scale(key, shape, pieces, -0.22, 0.18)
    return jnp.clip(array, -limit, limit).astype(held_as)


def setup_inputs(seed: int = 0, part: int = 0) -> dict:
    key_list = jax.random.split(jax.random.key(seed), 12)
    part_splits = jax.random.split(jax.random.fold_in(key_list[11], part), 12)
    return {
        "user_feats": gaussian(part_splits[0], (SLOTS, DH), 1.0, 6.0, ((0, 4),)),
        "user_slot": draw_user_slot(jax.random.fold_in(jax.random.fold_in(key_list[11], part), 71), part),
        "cand_pool": gaussian(part_splits[2], (POOL, DH), 1.0, 6.0),
        "cand_ids": with_ends(jax.random.randint(part_splits[3], (USERS, CANDS), 0, POOL), jax.random.fold_in(part_splits[3], 1), 0, POOL - 1).astype(jnp.int32),
        "first_weight": gaussian(key_list[4], (D, D), D ** -0.5, 0.0625, ((0, 4), (1, 4))),
        "first_bias": gaussian(key_list[5], (D,), 1.0, 5.0, ((0, 4),), jnp.float32),
        "second_weight": gaussian(key_list[6], (D, D), D ** -0.5, 0.0625, ((0, 4), (1, 4))),
        "second_bias": gaussian(key_list[7], (D,), 1.0, 5.0, ((0, 4),), jnp.float32),
        "third_weight": gaussian(key_list[8], (D, D), D ** -0.5, 0.0625, ((0, 4), (1, 4))),
        "third_bias": gaussian(key_list[9], (D,), 1.0, 5.0, ((0, 4),), jnp.float32),
        "score_weight": gaussian(key_list[10], (D,), D ** -0.5, 0.0625, ((0, 4),)),
    }


def reference(user_feats, user_slot, cand_pool, cand_ids, first_weight, first_bias, second_weight, second_bias, third_weight, third_bias, score_weight):
    user_rows = jnp.repeat(user_feats[user_slot], CANDS, axis=0)
    pool_rows = cand_pool[cand_ids.reshape(-1)]
    base = jnp.concatenate([user_rows, pool_rows], axis=1)
    first_sum = jnp.dot(base, first_weight, preferred_element_type=jnp.float32)
    cross_one = (base * (first_sum + first_bias) + base).astype(jnp.bfloat16)
    block = D // N_CAND
    second_sum = jnp.zeros((ROWS, D), jnp.float32)
    for piece in range(N_CAND):
        term = jnp.dot(cross_one[:, piece * block:(piece + 1) * block], second_weight[piece * block:(piece + 1) * block], preferred_element_type=jnp.float32)
        term = lax.optimization_barrier(term.astype(jnp.bfloat16))
        second_sum = second_sum + term.astype(jnp.float32)
    cross_two = (base * (second_sum + second_bias) + cross_one).astype(jnp.bfloat16)
    third_sum = jnp.dot(cross_two, third_weight, preferred_element_type=jnp.float32)
    cross_three = base * (third_sum + third_bias) + cross_two
    logits = jnp.sum(cross_three * score_weight.astype(jnp.float32), axis=1)
    return cross_three.astype(jnp.bfloat16), logits
```

```python
import jax
import jax.numpy as jnp
from jax import lax
from jax.sharding import PartitionSpec as P


F32 = jnp.float32
BF16 = jnp.bfloat16


def bits_of(count):
    bits, bit = [], 1
    while bit < count:
        bits.append(bit)
        bit *= 2
    assert bit == count
    return bits


def swap(value, axis, bit):
    count = lax.axis_size(axis)
    return lax.ppermute(value, axis, [(i, i ^ bit) for i in range(count)])


def pick(blocks, index, axis=0):
    return lax.dynamic_index_in_dim(blocks, index, axis, keepdims=False)


def bring_users(user_feats, user_slot):
    local = user_feats.shape[0]
    me = lax.axis_index("cand")
    rows = jnp.take(user_feats, user_slot % local, axis=0) if local > 1 else jnp.broadcast_to(
        user_feats, (user_slot.shape[0], user_feats.shape[1])
    )
    owner = user_slot // local
    for bit in bits_of(lax.axis_size("cand")):
        other = swap(rows, "cand", bit)
        rows = jnp.where((((owner ^ me) & bit) != 0)[:, None], other, rows)
    return rows


def sum_all(terms, axis):
    count = lax.axis_size(axis)
    bits = bits_of(count)
    low = lax.axis_index(axis) & 1
    halves = terms.reshape((2, terms.shape[0] // 2) + terms.shape[1:])
    total = pick(halves, low) + swap(pick(halves, 1 - low).astype(BF16), axis, 1).astype(F32)
    for bit in bits[1:]:
        total = total + swap(total.astype(BF16), axis, bit).astype(F32)
    return total, low


def join_halves(half, axis, low):
    other = swap(half, axis, 1)
    first = jnp.where(low == 0, half, other)
    second = jnp.where(low == 0, other, half)
    return jnp.concatenate([first, second], axis=0)


def scatter_low_first(terms, axis):
    count = lax.axis_size(axis)
    me = lax.axis_index(axis)
    blocks = terms.reshape((count, terms.shape[0] // count) + terms.shape[1:])
    for bit in bits_of(count):
        mine = (me // bit) % 2
        pairs = blocks.reshape((blocks.shape[0] // 2, 2) + blocks.shape[1:])
        blocks = pick(pairs, mine, 1) + swap(pick(pairs, 1 - mine, 1).astype(BF16), axis, bit).astype(F32)
    return blocks[0]


def scatter_direct(terms, axis):
    count = lax.axis_size(axis)
    if count > 4:
        return lax.psum_scatter(terms.astype(BF16), axis, scatter_dimension=0, tiled=True).astype(F32)
    me = lax.axis_index(axis)
    blocks = terms.reshape((count, terms.shape[0] // count) + terms.shape[1:])
    parts = [swap(pick(blocks, me ^ bit).astype(BF16), axis, bit) for bit in range(1, count)]
    total = pick(blocks, me)
    for part in parts:
        total = total + part.astype(F32)
    return total


def gather_direct(block, axis):
    count = lax.axis_size(axis)
    if count > 4:
        return lax.all_gather(block, axis, axis=0, tiled=True)
    me = lax.axis_index(axis)
    parts = jnp.stack([block] + [swap(block, axis, bit) for bit in range(1, count)])
    return jnp.concatenate([pick(parts, me ^ i) for i in range(count)], axis=0)


def overlap(have, have_index, want_width, want_index):
    rows, width = have.shape
    if width >= want_width:
        ratio = width // want_width
        inside = want_index // ratio == have_index
        piece = have
        if ratio > 1:
            piece = lax.dynamic_slice_in_dim(have, (want_index % ratio) * want_width, want_width, 1)
        return jnp.where(inside, piece, jnp.zeros_like(piece))
    ratio = want_width // width
    inside = have_index // ratio == want_index
    return lax.dynamic_update_slice_in_dim(
        jnp.zeros((rows, want_width), have.dtype),
        jnp.where(inside, have, jnp.zeros_like(have)),
        (have_index % ratio) * width,
        1,
    )


def body(
    user_feats,
    user_slot,
    cand_pool,
    cand_ids,
    first_weight,
    first_bias,
    second_weight,
    second_bias,
    third_weight,
    third_bias,
    score_weight,
):
    cand_count = lax.axis_size("cand")
    model_count = lax.axis_size("mp")
    cand_index = lax.axis_index("cand")
    model_index = lax.axis_index("mp")
    half_width = user_feats.shape[1]
    full_width = 2 * half_width
    user_count, per_user = cand_ids.shape
    row_total = user_count * per_user
    col_block = full_width // cand_count
    feat_block = full_width // model_count

    users = bring_users(user_feats, user_slot)
    chosen = (
        cand_ids.reshape(-1)[:, None]
        == lax.broadcasted_iota(jnp.int32, (row_total, cand_pool.shape[0]), 1)
    ).astype(BF16)
    owner = (
        lax.broadcasted_iota(jnp.int32, (row_total, user_count), 0) // per_user
        == lax.broadcasted_iota(jnp.int32, (row_total, user_count), 1)
    ).astype(BF16)

    def base_of(start, width):
        offset = start % half_width
        from_pool = jnp.dot(
            chosen,
            lax.dynamic_slice_in_dim(cand_pool, offset, width, 1),
            preferred_element_type=F32,
        )
        user_cols = lax.dynamic_slice_in_dim(users, offset, width, 1)
        if user_count == 1:
            from_users = user_cols.astype(F32)
        else:
            from_users = jnp.dot(owner, user_cols, preferred_element_type=F32)
        return jnp.where(start < half_width, from_users, from_pool).astype(BF16)

    base_model = base_of(model_index * feat_block, feat_block)
    base_cand = base_of(cand_index * col_block, col_block)

    terms_one = jnp.dot(base_model, first_weight, preferred_element_type=F32)
    sum_one, low = sum_all(terms_one, "mp")
    base_half = pick(base_cand.reshape(2, row_total // 2, col_block), low).astype(F32)
    cross_half = (base_half * (sum_one + first_bias) + base_half).astype(BF16)
    cross_one = join_halves(cross_half, "mp", low)

    terms_two = base_model * jnp.dot(cross_one, second_weight, preferred_element_type=F32)
    terms_two = terms_two + overlap(cross_one, cand_index, feat_block, model_index)
    local_rows = row_total // cand_count
    base_rows = lax.dynamic_slice_in_dim(base_model, cand_index * local_rows, local_rows, 0).astype(F32)
    cross_two = (scatter_direct(terms_two, "cand") + base_rows * second_bias).astype(BF16)
    cross_two = gather_direct(cross_two, "cand")

    terms_three = base_cand * jnp.dot(cross_two, third_weight, preferred_element_type=F32)
    terms_three = terms_three + overlap(cross_two, model_index, col_block, cand_index)
    row_block = row_total // model_count
    base_rows = lax.dynamic_slice_in_dim(base_cand, model_index * row_block, row_block, 0).astype(F32)
    cross_three = scatter_low_first(terms_three, "mp") + base_rows * third_bias

    logits = jnp.sum(cross_three * score_weight.astype(F32), axis=1)
    if cand_count <= 4:
        logits = sum([swap(logits, "cand", bit) for bit in range(1, cand_count)], logits)
    else:
        logits = lax.psum(logits, "cand")
    return (cross_three.astype(BF16), logits)


def solution(mesh):
    in_specs = (
        P(("groups", "cand"), None),
        P("groups"),
        P("groups", None),
        P("groups", None),
        P("mp", "cand"),
        P("cand"),
        P("cand", "mp"),
        P("mp"),
        P("mp", "cand"),
        P("cand"),
        P("cand"),
    )
    out_specs = (P(("groups", "mp"), "cand"), P(("groups", "mp")))
    return jax.shard_map(body, mesh=mesh, in_specs=in_specs, out_specs=out_specs, check_vma=False)
```

```python
import functools

import jax
import jax.numpy as jnp
from jax import lax
from jax.experimental import pallas as pl
from jax.experimental.pallas import tpu as pltpu
from jax.sharding import PartitionSpec as P


F32 = jnp.float32
BF16 = jnp.bfloat16
DIRECT = 4
MIB = 1024 * 1024


def bits_of(count):
    bits, bit = [], 1
    while bit < count:
        bits.append(bit)
        bit *= 2
    assert bit == count
    return bits


def swap(value, axis, bit):
    count = lax.axis_size(axis)
    return lax.ppermute(value, axis, [(i, i ^ bit) for i in range(count)])


def call(kernel, outs, args, smem=(), scratch=(), flops=0, limit=6 * MIB):
    moved = sum(a.size * a.dtype.itemsize for a in args if a.size < 2 * MIB)
    moved += sum(functools.reduce(lambda a, b: a * b, s) * jnp.dtype(d).itemsize for s, d in outs)
    return pl.pallas_call(
        kernel,
        name=(kernel.func if isinstance(kernel, functools.partial) else kernel).__name__,
        out_shape=[jax.ShapeDtypeStruct(s, d) for s, d in outs],
        in_specs=[
            pl.BlockSpec(memory_space=pltpu.SMEM if i in smem else pltpu.VMEM)
            for i in range(len(args))
        ],
        out_specs=[pl.BlockSpec(memory_space=pltpu.VMEM)] * len(outs),
        scratch_shapes=list(scratch),
        compiler_params=pltpu.CompilerParams(vmem_limit_bytes=limit),
        cost_estimate=pl.CostEstimate(flops=flops, bytes_accessed=moved, transcendentals=0),
    )(*args)


def aligned(index, size):
    return pl.ds(pl.multiple_of(index * size, size), size)


def from_owner(slot_ref, local, bit, own, other):
    me = lax.axis_index("cand")
    row = lax.broadcasted_iota(jnp.int32, own.shape, 0)
    differs = jnp.zeros(own.shape, jnp.int32)
    for user in range(own.shape[0]):
        here = ((slot_ref[user] // local) ^ me) & bit
        differs = jnp.where(row == user, here, differs)
    return jnp.where(differs != 0, other.astype(F32), own.astype(F32))


def choose_user(local, bit, slot_ref, own_ref, other_ref, out_ref):
    out_ref[...] = from_owner(slot_ref, local, bit, own_ref[...], other_ref[...]).astype(BF16)


def choose_pool(half, ids_ref, pool_ref, model_ref, cand_ref):
    users, rows = ids_ref.shape
    numbers = lax.broadcasted_iota(jnp.int32, (pool_ref.shape[0], rows), 0)
    for axis, out_ref in (("mp", model_ref), ("cand", cand_ref)):
        width = out_ref.shape[1]
        cols = aligned(lax.axis_index(axis) % (half // width), width)
        for user in range(users):
            chosen = (numbers == ids_ref[pl.ds(user, 1), :]).astype(BF16)
            out_ref[pl.ds(user * rows, rows), :] = lax.dot_general(
                chosen, pool_ref[:, cols], (((0,), (0,)), ((), ())), preferred_element_type=F32
            ).astype(BF16)


def tiles(width, step=512):
    step = min(step, width)
    return [pl.ds(i, step) for i in range(0, width, step)]


def multiply(rows_ref, weight_ref, out_ref, scale_ref=None):
    for cols in tiles(out_ref.shape[1]):
        value = jnp.dot(rows_ref[...], weight_ref[:, cols], preferred_element_type=F32)
        out_ref[:, cols] = value if scale_ref is None else scale_ref[:, cols].astype(F32) * value


def layer_one(
    half, local, bit, slot_ref, own_ref, other_ref, pool_model_ref, pool_cand_ref, weight_ref,
    model_ref, cand_ref, keep_ref, send_ref, terms_ref,
):
    users = own_ref.shape[0]
    for axis, pool_ref, out_ref in (
        ("mp", pool_model_ref, model_ref),
        ("cand", pool_cand_ref, cand_ref),
    ):
        rows, width = out_ref.shape
        block = lax.axis_index(axis)
        inside = block < half // width

        @pl.when(inside)
        def _():
            cols = aligned(block % (half // width), width)
            chosen = from_owner(slot_ref, local, bit, own_ref[:, cols], other_ref[:, cols])
            for user in range(users):
                out_ref[pl.ds(user * (rows // users), rows // users), :] = jnp.broadcast_to(
                    chosen[user : user + 1], (rows // users, width)
                ).astype(BF16)

        @pl.when(jnp.logical_not(inside))
        def _():
            out_ref[...] = pool_ref[...]

    multiply(model_ref, weight_ref, terms_ref)
    low = lax.axis_index("mp") % 2
    size = keep_ref.shape[0]
    keep_ref[...] = terms_ref[aligned(low, size), :]
    send_ref[...] = terms_ref[aligned(1 - low, size), :].astype(BF16)


def add_up(keep_ref, other_ref, sum_ref, send_ref):
    total = keep_ref[...] + other_ref[...].astype(F32)
    sum_ref[...] = total
    send_ref[...] = total.astype(BF16)


def cross_half(sum_ref, other_ref, base_ref, bias_ref, out_ref):
    size = out_ref.shape[0]
    base = base_ref[aligned(lax.axis_index("mp") % 2, size), :].astype(F32)
    total = sum_ref[...] + other_ref[...].astype(F32)
    out_ref[...] = (base * (total + bias_ref[...]) + base).astype(BF16)


def add_own_columns(terms_ref, rows_ref, have, want):
    width, wanted = rows_ref.shape[1], terms_ref.shape[1]
    small = min(width, wanted)
    ratio = max(width, wanted) // small
    assert max(width, wanted) == ratio * small
    if width >= wanted:
        inside, here, there = want // ratio == have, aligned(want % ratio, small), slice(None)
    else:
        inside, here, there = have // ratio == want, slice(None), aligned(have % ratio, small)

    @pl.when(inside)
    def _():
        terms_ref[:, there] += rows_ref[:, here].astype(F32)


def layer_two(mine_ref, other_ref, base_ref, weight_ref, *refs):
    *out_refs, rows_ref, terms_ref = refs
    low = lax.axis_index("mp") % 2
    size = mine_ref.shape[0]
    rows_ref[aligned(low, size), :] = mine_ref[...]
    rows_ref[aligned(1 - low, size), :] = other_ref[...]
    multiply(rows_ref, weight_ref, terms_ref, base_ref)
    cand = lax.axis_index("cand")
    add_own_columns(terms_ref, rows_ref, cand, lax.axis_index("mp"))
    if len(out_refs) == 1:
        out_refs[0][...] = terms_ref[...].astype(BF16)
        return
    for bit, out_ref in enumerate(out_refs):
        out_ref[...] = terms_ref[aligned(cand ^ bit, out_ref.shape[0]), :].astype(out_ref.dtype)


def cross_rows(count, base_ref, bias_ref, *refs):
    *part_refs, out_ref = refs
    total = part_refs[0][...].astype(F32)
    for part_ref in part_refs[1:]:
        total = total + part_ref[...].astype(F32)
    base = base_ref[aligned(lax.axis_index("cand"), out_ref.shape[0]), :].astype(F32)
    out_ref[...] = (total + base * bias_ref[...]).astype(BF16)


def split_low(axis_bit, terms_ref, keep_ref, send_ref, size):
    for pair in range(keep_ref.shape[0] // size):
        rows = pl.ds(pair * size, size)
        keep_ref[rows, :] = terms_ref[aligned(2 * pair + axis_bit, size), :]
        send_ref[rows, :] = terms_ref[aligned(2 * pair + 1 - axis_bit, size), :].astype(BF16)


def layer_three(row_block, base_ref, weight_ref, *refs):
    *part_refs, keep_ref, send_ref, rows_ref, terms_ref = refs
    cand = lax.axis_index("cand")
    if len(part_refs) == 1:
        rows_ref[...] = part_refs[0][...]
    else:
        for bit, part_ref in enumerate(part_refs):
            rows_ref[aligned(cand ^ bit, part_ref.shape[0]), :] = part_ref[...]
    multiply(rows_ref, weight_ref, terms_ref, base_ref)
    model = lax.axis_index("mp")
    add_own_columns(terms_ref, rows_ref, model, cand)
    split_low(model % 2, terms_ref, keep_ref, send_ref, row_block)


def halve(row_block, bit, keep_ref, other_ref, kept_ref, send_ref, terms_ref):
    terms_ref[...] = keep_ref[...] + other_ref[...].astype(F32)
    split_low((lax.axis_index("mp") // bit) % 2, terms_ref, kept_ref, send_ref, row_block)


def finish(keep_ref, other_ref, base_ref, bias_ref, score_ref, out_ref, logit_ref):
    base = base_ref[aligned(lax.axis_index("mp"), out_ref.shape[0]), :].astype(F32)
    cross = keep_ref[...] + other_ref[...].astype(F32) + base * bias_ref[...]
    out_ref[...] = cross.astype(BF16)
    logit_ref[...] = jnp.sum(cross * score_ref[...].astype(F32), axis=1, keepdims=True)


def body(
    user_feats,
    user_slot,
    cand_pool,
    cand_ids,
    first_weight,
    first_bias,
    second_weight,
    second_bias,
    third_weight,
    third_bias,
    score_weight,
):
    cand_count = lax.axis_size("cand")
    model_count = lax.axis_size("mp")
    local, half_width = user_feats.shape
    full_width = 2 * half_width
    user_count, per_user = cand_ids.shape
    row_total = user_count * per_user
    col_block = full_width // cand_count
    feat_block = full_width // model_count
    local_rows = row_total // cand_count
    row_block = row_total // model_count
    half_rows = row_total // 2
    flops = 2 * row_total * col_block * feat_block
    direct = cand_count <= DIRECT

    pool_model, pool_cand = call(
        functools.partial(choose_pool, half_width),
        [((row_total, feat_block), BF16), ((row_total, col_block), BF16)],
        [cand_ids, cand_pool],
        limit=8 * MIB,
    )

    if local > 1:
        users = jnp.take(user_feats, user_slot % local, axis=0)
    else:
        users = jnp.broadcast_to(user_feats, (user_count, half_width))
    *bits, last_bit = bits_of(cand_count)
    for bit in bits:
        (users,) = call(
            functools.partial(choose_user, local, bit),
            [((user_count, half_width), BF16)],
            [user_slot, users, swap(users, "cand", bit)],
            smem=(0,),
        )

    base_model, base_cand, keep, send = call(
        functools.partial(layer_one, half_width, local, last_bit),
        [
            ((row_total, feat_block), BF16),
            ((row_total, col_block), BF16),
            ((half_rows, col_block), F32),
            ((half_rows, col_block), BF16),
        ],
        [user_slot, users, swap(users, "cand", last_bit), pool_model, pool_cand, first_weight],
        smem=(0,),
        scratch=[pltpu.VMEM((row_total, col_block), F32)],
        flops=flops,
        limit=12 * MIB,
    )
    other = swap(send, "mp", 1)
    for bit in bits_of(model_count)[1:]:
        keep, send = call(
            add_up, [((half_rows, col_block), F32), ((half_rows, col_block), BF16)], [keep, other]
        )
        other = swap(send, "mp", bit)
    (mine,) = call(
        cross_half,
        [((half_rows, col_block), BF16)],
        [keep, other, base_cand, first_bias.reshape(1, -1)],
    )

    if direct:
        outs = [((local_rows, feat_block), BF16 if bit else F32) for bit in range(cand_count)]
    else:
        outs = [((row_total, feat_block), BF16)]
    parts = call(
        layer_two,
        outs,
        [mine, swap(mine, "mp", 1), base_model, second_weight],
        scratch=[pltpu.VMEM((row_total, col_block), BF16), pltpu.VMEM((row_total, feat_block), F32)],
        flops=flops,
        limit=12 * MIB,
    )
    if direct:
        parts = [parts[0]] + [swap(parts[bit], "cand", bit) for bit in range(1, cand_count)]
    else:
        parts = [lax.psum_scatter(parts[0], "cand", scatter_dimension=0, tiled=True)]
    (block,) = call(
        functools.partial(cross_rows, cand_count),
        [((local_rows, feat_block), BF16)],
        [base_model, second_bias.reshape(1, -1), *parts],
    )
    if direct:
        parts = [block] + [swap(block, "cand", bit) for bit in range(1, cand_count)]
    else:
        parts = [lax.all_gather(block, "cand", axis=0, tiled=True)]

    rows = row_total // 2
    keep, send = call(
        functools.partial(layer_three, row_block),
        [((rows, col_block), F32), ((rows, col_block), BF16)],
        [base_cand, third_weight, *parts],
        scratch=[pltpu.VMEM((row_total, feat_block), BF16), pltpu.VMEM((row_total, col_block), F32)],
        flops=flops,
        limit=12 * MIB,
    )
    other = swap(send, "mp", 1)
    for bit in bits_of(model_count)[1:]:
        scratch = [pltpu.VMEM((rows, col_block), F32)]
        rows //= 2
        keep, send = call(
            functools.partial(halve, row_block, bit),
            [((rows, col_block), F32), ((rows, col_block), BF16)],
            [keep, other],
            scratch=scratch,
        )
        other = swap(send, "mp", bit)
    crossed, logits = call(
        finish,
        [((row_block, col_block), BF16), ((row_block, 1), F32)],
        [keep, other, base_cand, third_bias.reshape(1, -1), score_weight.reshape(1, -1)],
    )
    if direct:
        logits = sum([swap(logits, "cand", bit) for bit in range(1, cand_count)], logits)
    else:
        logits = lax.psum(logits, "cand")
    return (crossed, logits.reshape(-1))


def solution(mesh):
    in_specs = (
        P(("groups", "cand"), None),
        P("groups"),
        P("groups", None),
        P("groups", None),
        P("mp", "cand"),
        P("cand"),
        P("cand", "mp"),
        P("mp"),
        P("mp", "cand"),
        P("cand"),
        P("cand"),
    )
    out_specs = (P(("groups", "mp"), "cand"), P(("groups", "mp")))
    return jax.shard_map(body, mesh=mesh, in_specs=in_specs, out_specs=out_specs, check_vma=False)
```

```python
import functools

import jax
import jax.numpy as jnp
from jax import lax
from jax.experimental import pallas as pl
from jax.experimental.pallas import tpu as pltpu
from jax.sharding import PartitionSpec as P


F32 = jnp.float32
BF16 = jnp.bfloat16
LANES = 128
DIRECT = 4
MIB = 1024 * 1024
STAGE_FLOPS = 1 << 34


def bits_of(count):
    bits, bit = [], 1
    while bit < count:
        bits.append(bit)
        bit *= 2
    assert bit == count
    return bits


def swap(value, axis, bit):
    count = lax.axis_size(axis)
    return lax.ppermute(value, axis, [(i, i ^ bit) for i in range(count)])


def call(kernel, outs, args, scratch=(), hbm=(), smem=(), flops=0, limit=6 * MIB):
    moved = sum(a.size * a.dtype.itemsize for a in args if a.size < 2 * MIB)
    moved += sum(functools.reduce(lambda a, b: a * b, s) * jnp.dtype(d).itemsize for s, d in outs)
    return pl.pallas_call(
        kernel,
        out_shape=[jax.ShapeDtypeStruct(s, d) for s, d in outs],
        in_specs=[
            pl.BlockSpec(
                memory_space=pltpu.HBM if i in hbm else pltpu.SMEM if i in smem else pltpu.VMEM
            )
            for i in range(len(args))
        ],
        out_specs=[pl.BlockSpec(memory_space=pltpu.VMEM)] * len(outs),
        scratch_shapes=list(scratch),
        compiler_params=pltpu.CompilerParams(vmem_limit_bytes=limit),
        cost_estimate=pl.CostEstimate(flops=flops, bytes_accessed=moved, transcendentals=0),
    )(*[pltpu.with_memory_space_constraint(a, pltpu.HBM) if i in hbm else a for i, a in enumerate(args)])


def aligned(index, size):
    return pl.ds(pl.multiple_of(index * size, size), size)


def add_to(*refs):
    *part_refs, out_ref = refs
    total = part_refs[0][...]
    for part_ref in part_refs[1:]:
        total = total + part_ref[...]
    out_ref[...] = total


def stage(out_ref):
    out_ref[...] = jnp.zeros_like(out_ref)


def choose_user(local, bit, slot_ref, own_ref, other_ref, out_ref):
    want = (slot_ref[...] // local) ^ lax.axis_index("cand")
    other, own = other_ref[...].astype(F32), own_ref[...].astype(F32)
    out_ref[...] = jnp.where((jnp.broadcast_to(want, own.shape) & bit) != 0, other, own).astype(BF16)


def owner_steps(local, slot_ref, out_ref):
    row = lax.broadcasted_iota(jnp.int32, out_ref.shape, 0)
    want = jnp.zeros(out_ref.shape, jnp.int32)
    for user in range(out_ref.shape[0]):
        owner = lax.div(slot_ref[user], local) ^ lax.axis_index("cand")
        want = jnp.where(row == user, owner, want)
    out_ref[...] = want


def choose_pool(
    half, ids_ref, pool_ref, _, model_ref, cand_ref
):
    users, rows = ids_ref.shape
    numbers = lax.broadcasted_iota(jnp.int32, (pool_ref.shape[0], rows), 0)
    for axis, out_ref in (("mp", model_ref), ("cand", cand_ref)):
        width = out_ref.shape[1]
        cols = aligned(lax.axis_index(axis) % (half // width), width)
        for user in range(users):
            chosen = (numbers == ids_ref[pl.ds(user, 1), :]).astype(BF16)
            out_ref[pl.ds(user * rows, rows), :] = lax.dot_general(
                chosen, pool_ref[:, cols], (((0,), (0,)), ((), ())), preferred_element_type=F32
            ).astype(BF16)


def tiles(width, step=512):
    step = min(step, width)
    return [pl.ds(i, step) for i in range(0, width, step)]


def multiply(rows_ref, weight_ref, out_ref, scale_ref=None):
    for cols in tiles(out_ref.shape[1]):
        value = jnp.dot(rows_ref[...], weight_ref[:, cols], preferred_element_type=F32)
        out_ref[:, cols] = value if scale_ref is None else scale_ref[:, cols].astype(F32) * value


def pool_terms(half, rows_ref, weight_ref, keep_ref, send_ref, terms_ref):
    inside = lax.axis_index("mp") < half // rows_ref.shape[1]

    @pl.when(inside)
    def _():
        keep_ref[...] = jnp.zeros_like(keep_ref)
        send_ref[...] = jnp.zeros_like(send_ref)

    @pl.when(jnp.logical_not(inside))
    def _():
        multiply(rows_ref, weight_ref, terms_ref)
        low = lax.axis_index("mp") % 2
        size = keep_ref.shape[0]
        keep_ref[...] = terms_ref[aligned(low, size), :]
        send_ref[...] = terms_ref[aligned(1 - low, size), :].astype(BF16)


def user_terms(
    half, want_ref, weight_ref, pool_model_ref, pool_cand_ref, *refs
):
    *part_refs, model_ref, cand_ref, terms_ref = refs
    users = part_refs[0].shape[0]
    terms_ref[...] = jnp.zeros_like(terms_ref)
    for axis, pool_ref, out_ref in (
        ("mp", pool_model_ref, model_ref),
        ("cand", pool_cand_ref, cand_ref),
    ):
        rows, width = out_ref.shape
        block = lax.axis_index(axis)
        inside = block < half // width

        @pl.when(inside)
        def _():
            cols = aligned(block % (half // width), width)
            parts = [part_ref[:, cols] for part_ref in part_refs]
            chosen = parts[0].astype(F32)
            want = jnp.broadcast_to(want_ref[:, :1], chosen.shape)
            for bit in range(1, len(parts)):
                chosen = jnp.where(want == bit, parts[bit].astype(F32), chosen)
            for user in range(users):
                out_ref[pl.ds(user * (rows // users), rows // users), :] = jnp.broadcast_to(
                    chosen[user : user + 1], (rows // users, width)
                ).astype(BF16)
            if axis == "mp":
                padded = chosen
                if users < 8:
                    padded = jnp.concatenate([chosen, jnp.zeros((8 - users, width), F32)], axis=0)
                padded = padded.astype(BF16)
                for tile in tiles(terms_ref.shape[1]):
                    value = jnp.dot(padded, weight_ref[:, tile], preferred_element_type=F32)
                    terms_ref[:, tile] = value[:users]

        @pl.when(jnp.logical_not(inside))
        def _():
            out_ref[...] = pool_ref[...]


def add_up(keep_ref, other_ref, sum_ref, send_ref):
    total = keep_ref[...] + other_ref[...].astype(F32)
    sum_ref[...] = total
    send_ref[...] = total.astype(BF16)


def add_own_columns(terms_ref, rows_ref, have, want):
    width, wanted = rows_ref.shape[1], terms_ref.shape[1]
    small = min(width, wanted)
    ratio = max(width, wanted) // small
    assert max(width, wanted) == ratio * small
    if width >= wanted:
        inside, here, there = want // ratio == have, aligned(want % ratio, small), slice(None)
    else:
        inside, here, there = have // ratio == want, slice(None), aligned(have % ratio, small)

    @pl.when(inside)
    def _():
        terms_ref[:, there] += rows_ref[:, here].astype(F32)


def layer_two(
    mine_ref, other_ref, user_ref, user_other_ref, bias_ref, cand_ref, base_ref, weight_ref, *refs
):
    *out_refs, rows_ref, terms_ref, user_sum_ref = refs
    low = lax.axis_index("mp") % 2
    size = mine_ref.shape[0]
    users = user_ref.shape[0]
    assert users == 1 or users % 2 == 0
    user_sum_ref[...] = user_ref[...] + user_other_ref[...] + bias_ref[...]
    each = max(users // 2, 1)
    for index, pool_ref in ((low, mine_ref), (1 - low, other_ref)):
        for piece in range(each):
            user = index * each + piece if users > 1 else 0
            part = pl.ds(piece * (size // each), size // each)
            here = aligned(index * each + piece, size // each)
            base = cand_ref[here, :].astype(F32)
            total = pool_ref[part, :].astype(F32) + user_sum_ref[pl.ds(user, 1), :]
            rows_ref[here, :] = (base * total + base).astype(BF16)
    multiply(rows_ref, weight_ref, terms_ref, base_ref)
    cand = lax.axis_index("cand")
    add_own_columns(terms_ref, rows_ref, cand, lax.axis_index("mp"))
    if len(out_refs) == 1:
        out_refs[0][...] = terms_ref[...].astype(BF16)
        return
    for bit, out_ref in enumerate(out_refs):
        out_ref[...] = terms_ref[aligned(cand ^ bit, out_ref.shape[0]), :].astype(out_ref.dtype)


def cross_rows(base_ref, bias_ref, *refs):
    *part_refs, out_ref = refs
    total = part_refs[0][...].astype(F32)
    for part_ref in part_refs[1:]:
        total = total + part_ref[...].astype(F32)
    base = base_ref[aligned(lax.axis_index("cand"), out_ref.shape[0]), :].astype(F32)
    out_ref[...] = (total + base * bias_ref[...]).astype(BF16)


def split_low(axis_bit, terms_ref, keep_ref, send_ref, size):
    for pair in range(keep_ref.shape[0] // size):
        rows = pl.ds(pair * size, size)
        keep_ref[rows, :] = terms_ref[aligned(2 * pair + axis_bit, size), :]
        send_ref[rows, :] = terms_ref[aligned(2 * pair + 1 - axis_bit, size), :].astype(BF16)


def score_map(base_ref, score_ref, weight_ref, out_ref, rows_ref, score_row_ref):
    rows_ref[...] = (base_ref[...].astype(F32) * score_ref[...].astype(F32)).astype(BF16)
    for part in tiles(out_ref.shape[1]):
        out_ref[:, part] = lax.dot_general(
            rows_ref[...], weight_ref[part, :], (((1,), (1,)), ((), ())), preferred_element_type=F32
        )
    score_row_ref[...] = jnp.broadcast_to(score_ref[...].astype(F32), score_row_ref.shape)
    add_own_columns(out_ref, score_row_ref, lax.axis_index("cand"), lax.axis_index("mp"))


def score_rows(map_ref, base_ref, bias_ref, score_ref, *refs):
    *part_refs, rows_ref, logit_ref = refs
    cand = lax.axis_index("cand")
    if len(part_refs) == 1:
        rows_ref[...] = part_refs[0][...]
    else:
        for bit, part_ref in enumerate(part_refs):
            rows_ref[aligned(cand ^ bit, part_ref.shape[0]), :] = part_ref[...]
    once = (lax.axis_index("mp") == 0).astype(F32)
    blocks, size = logit_ref.shape
    lanes = 128
    for block in range(blocks):
        rows = pl.ds(block * size, size)
        total = jnp.zeros((size, lanes), F32)
        for start in range(0, map_ref.shape[1], lanes):
            cols = pl.ds(start, lanes)
            total = total + rows_ref[rows, cols].astype(F32) * map_ref[rows, cols]
        for start in range(0, base_ref.shape[1], lanes):
            cols = pl.ds(start, lanes)
            weight = bias_ref[:, cols] * score_ref[:, cols].astype(F32) * once
            total = total + base_ref[rows, cols].astype(F32) * weight
        logit_ref[pl.ds(block, 1), :] = jnp.sum(total.T, axis=0, keepdims=True)


def layer_three(row_block, base_ref, weight_ref, rows_ref, keep_ref, send_ref, terms_ref):
    multiply(rows_ref, weight_ref, terms_ref, base_ref)
    model = lax.axis_index("mp")
    add_own_columns(terms_ref, rows_ref, model, lax.axis_index("cand"))
    split_low(model % 2, terms_ref, keep_ref, send_ref, row_block)


def halve(row_block, bit, keep_ref, other_ref, kept_ref, send_ref, terms_ref):
    terms_ref[...] = keep_ref[...] + other_ref[...].astype(F32)
    split_low((lax.axis_index("mp") // bit) % 2, terms_ref, kept_ref, send_ref, row_block)


def halve_last(
    bit, keep_ref, other_ref, total_ref, part_ref, kept_ref, send_ref, sum_ref, terms_ref, tile_ref
):
    terms_ref[...] = keep_ref[...] + other_ref[...].astype(F32)
    mine = (lax.axis_index("mp") // bit) % 2
    size, width = kept_ref.shape
    kept_ref[...] = terms_ref[aligned(mine, size), :]
    send_ref[:, pl.ds(0, width)] = terms_ref[aligned(1 - mine, size), :].astype(BF16)
    blocks, each = total_ref.shape
    rest = total_ref[...] + part_ref[...]
    sum_ref[...] = rest
    tile_ref[...] = jnp.zeros_like(tile_ref)
    for piece in range(3):
        rounded = rest.astype(BF16).astype(F32)
        tile_ref[pl.ds(piece * blocks, blocks), pl.ds(0, each)] = rounded
        rest = rest - rounded
    send_ref[:, pl.ds(width, LANES)] = tile_ref[...].astype(BF16)


def finish(keep_ref, other_ref, base_ref, bias_ref, total_ref, out_ref, logit_ref, tile_ref):
    model = lax.axis_index("mp")
    size, width = keep_ref.shape
    base = base_ref[aligned(model, size), :].astype(F32)
    cross = keep_ref[...] + other_ref[:, pl.ds(0, width)].astype(F32) + base * bias_ref[...]
    out_ref[...] = cross.astype(BF16)
    tile_ref[...] = other_ref[:, pl.ds(width, LANES)].astype(F32)
    blocks, each = total_ref.shape
    total = total_ref[pl.ds(model, 1), :]
    for piece in range(3):
        total = total + tile_ref[pl.ds(piece * blocks + model, 1), :][:, :each]
    logit_ref[...] = total


def body(
    user_feats,
    user_slot,
    cand_pool,
    cand_ids,
    first_weight,
    first_bias,
    second_weight,
    second_bias,
    third_weight,
    third_bias,
    score_weight,
):
    cand_count = lax.axis_size("cand")
    model_count = lax.axis_size("mp")
    local, half_width = user_feats.shape
    full_width = 2 * half_width
    user_count, per_user = cand_ids.shape
    row_total = user_count * per_user
    col_block = full_width // cand_count
    feat_block = full_width // model_count
    local_rows = row_total // cand_count
    row_block = row_total // model_count
    half_rows = row_total // 2
    flops = 2 * row_total * col_block * feat_block
    direct = cand_count <= DIRECT

    if local > 1:
        user_feats = jnp.take(user_feats, user_slot % local, axis=0)
    elif user_count > 1:
        user_feats = jnp.broadcast_to(user_feats, (user_count, half_width))
    (staged,) = call(stage, [((8, 128), F32)], [], flops=STAGE_FLOPS)
    users = user_feats
    pool_model, pool_cand = call(
        functools.partial(choose_pool, half_width),
        [
            ((row_total, feat_block), BF16),
            ((row_total, col_block), BF16),
        ],
        [cand_ids, cand_pool, staged],
        limit=8 * MIB,
    )
    (want,) = call(
        functools.partial(owner_steps, local),
        [((user_count, 128), jnp.int32)],
        [user_slot],
        smem=(0,),
    )
    if direct:
        users = [users] + [swap(users, "cand", bit) for bit in range(1, cand_count)]
    else:
        slots = user_slot.reshape(-1, 1)
        for bit in bits_of(cand_count):
            (users,) = call(
                functools.partial(choose_user, local, bit),
                [((user_count, half_width), BF16)],
                [slots, users, swap(users, "cand", bit)],
            )
        users = [users]

    half_outs = [((half_rows, col_block), F32), ((half_rows, col_block), BF16)]
    keep, send = call(
        functools.partial(pool_terms, half_width),
        half_outs,
        [pool_model, first_weight],
        scratch=[pltpu.VMEM((row_total, col_block), F32)],
        flops=flops,
        limit=12 * MIB,
    )
    for bit in bits_of(model_count):
        keep, send = call(add_up, half_outs, [keep, swap(send, "mp", bit)])
    pool_other = swap(send, "mp", 1)

    base_model, base_cand, user_sum = call(
        functools.partial(user_terms, half_width),
        [
            ((row_total, feat_block), BF16),
            ((row_total, col_block), BF16),
            ((user_count, col_block), F32),
        ],
        [want, first_weight, pool_model, pool_cand, *users],
        flops=flops,
        limit=12 * MIB,
    )
    *bits, last_bit = bits_of(model_count)
    for bit in bits:
        other = swap(user_sum, "mp", bit)
        (user_sum,) = call(add_to, [((user_count, col_block), F32)], [user_sum, other])
    user_other = swap(user_sum, "mp", last_bit)

    if direct:
        outs = [((local_rows, feat_block), BF16 if bit else F32) for bit in range(cand_count)]
    else:
        outs = [((row_total, feat_block), BF16)]
    parts = call(
        layer_two,
        outs,
        [
            keep, pool_other, user_sum, user_other, first_bias.reshape(1, -1), base_cand,
            base_model, second_weight,
        ],
        scratch=[
            pltpu.VMEM((row_total, col_block), BF16),
            pltpu.VMEM((row_total, feat_block), F32),
            pltpu.VMEM((user_count, col_block), F32),
        ],
        flops=flops,
        limit=12 * MIB,
    )
    if direct:
        parts = [parts[0]] + [swap(parts[bit], "cand", bit) for bit in range(1, cand_count)]
    else:
        parts = [lax.psum_scatter(parts[0], "cand", scatter_dimension=0, tiled=True)]
    score = score_weight.reshape(1, -1)
    (mapped,) = call(
        score_map,
        [((row_total, feat_block), F32)],
        [base_cand, score, third_weight],
        scratch=[pltpu.VMEM((row_total, col_block), BF16), pltpu.VMEM((row_total, col_block), F32)],
        flops=flops,
        limit=12 * MIB,
    )
    (block,) = call(
        cross_rows,
        [((local_rows, feat_block), BF16)],
        [base_model, second_bias.reshape(1, -1), *parts],
    )
    if direct:
        parts = [block] + [swap(block, "cand", bit) for bit in range(1, cand_count)]
    else:
        parts = [lax.all_gather(block, "cand", axis=0, tiled=True)]

    bias = third_bias.reshape(1, -1)
    logit_out = [((model_count, row_block), F32)]
    cross_two, logits = call(
        score_rows,
        [((row_total, feat_block), BF16)] + logit_out,
        [mapped, base_cand, bias, score, *parts],
    )
    rows = row_total // 2
    keep, send = call(
        functools.partial(layer_three, row_block),
        [((rows, col_block), F32), ((rows, col_block), BF16)],
        [base_cand, third_weight, cross_two],
        scratch=[pltpu.VMEM((row_total, col_block), F32)],
        flops=flops,
        limit=12 * MIB,
    )
    if direct:
        others = [swap(logits, "cand", bit) for bit in range(1, cand_count)]
        (logits,) = call(add_to, logit_out, [logits, *others])
    else:
        for bit in bits_of(cand_count):
            (logits,) = call(add_to, logit_out, [logits, swap(logits, "cand", bit)])
    *bits, last_bit = bits_of(model_count)
    assert bits and 3 * model_count <= row_block <= LANES
    other = swap(send, "mp", 1)
    logits_other = swap(logits, "mp", 1)
    for bit in bits[1:]:
        scratch = [pltpu.VMEM((rows, col_block), F32)]
        rows //= 2
        keep, send = call(
            functools.partial(halve, row_block, bit),
            [((rows, col_block), F32), ((rows, col_block), BF16)],
            [keep, other],
            scratch=scratch,
        )
        other = swap(send, "mp", bit)
        (logits,) = call(add_to, logit_out, [logits, logits_other])
        logits_other = swap(logits, "mp", bit)
    tile = pltpu.VMEM((row_block, LANES), F32)
    keep, send, logits = call(
        functools.partial(halve_last, last_bit),
        [((row_block, col_block), F32), ((row_block, col_block + LANES), BF16)] + logit_out,
        [keep, other, logits, logits_other],
        scratch=[pltpu.VMEM((rows, col_block), F32), tile],
    )
    crossed, logits = call(
        finish,
        [((row_block, col_block), BF16), ((1, row_block), F32)],
        [keep, swap(send, "mp", last_bit), base_cand, bias, logits],
        scratch=[tile],
    )
    return (crossed, logits.reshape(-1))


def solution(mesh):
    in_specs = (
        P(("groups", "cand"), None),
        P("groups"),
        P("groups", None),
        P("groups", None),
        P("mp", "cand"),
        P("cand"),
        P("cand", "mp"),
        P("mp"),
        P("mp", "cand"),
        P("cand"),
        P("cand"),
    )
    out_specs = (P(("groups", "mp"), "cand"), P(("groups", "mp")))

    return jax.shard_map(body, mesh=mesh, in_specs=in_specs, out_specs=out_specs, check_vma=False)
```

```python
import functools

import jax
import jax.numpy as jnp
from jax import lax
from jax.experimental import pallas as pl
from jax.experimental.pallas import tpu as pltpu
from jax.sharding import PartitionSpec as P


F32 = jnp.float32
BF16 = jnp.bfloat16
DIRECT = 4
MIB = 1024 * 1024
STAGE_FLOPS = 1 << 34


def bits_of(count):
    bits, bit = [], 1
    while bit < count:
        bits.append(bit)
        bit *= 2
    assert bit == count
    return bits


def swap(value, axis, bit):
    count = lax.axis_size(axis)
    return lax.ppermute(value, axis, [(i, i ^ bit) for i in range(count)])


def call(kernel, outs, args, scratch=(), hbm=(), smem=(), flops=0, limit=6 * MIB):
    moved = sum(a.size * a.dtype.itemsize for a in args if a.size < 2 * MIB)
    moved += sum(functools.reduce(lambda a, b: a * b, s) * jnp.dtype(d).itemsize for s, d in outs)
    return pl.pallas_call(
        kernel,
        out_shape=[jax.ShapeDtypeStruct(s, d) for s, d in outs],
        in_specs=[
            pl.BlockSpec(
                memory_space=pltpu.HBM if i in hbm else pltpu.SMEM if i in smem else pltpu.VMEM
            )
            for i in range(len(args))
        ],
        out_specs=[pl.BlockSpec(memory_space=pltpu.VMEM)] * len(outs),
        scratch_shapes=list(scratch),
        compiler_params=pltpu.CompilerParams(vmem_limit_bytes=limit),
        cost_estimate=pl.CostEstimate(flops=flops, bytes_accessed=moved, transcendentals=0),
    )(*[pltpu.with_memory_space_constraint(a, pltpu.HBM) if i in hbm else a for i, a in enumerate(args)])


def aligned(index, size):
    return pl.ds(pl.multiple_of(index * size, size), size)


def add_to(*refs):
    *part_refs, out_ref = refs
    total = part_refs[0][...]
    for part_ref in part_refs[1:]:
        total = total + part_ref[...]
    out_ref[...] = total


def stage(out_ref):
    out_ref[...] = jnp.zeros_like(out_ref)


def choose_user(local, bit, slot_ref, own_ref, other_ref, out_ref):
    want = (slot_ref[...] // local) ^ lax.axis_index("cand")
    other, own = other_ref[...].astype(F32), own_ref[...].astype(F32)
    out_ref[...] = jnp.where((jnp.broadcast_to(want, own.shape) & bit) != 0, other, own).astype(BF16)


def owner_steps(local, slot_ref, out_ref):
    row = lax.broadcasted_iota(jnp.int32, out_ref.shape, 0)
    want = jnp.zeros(out_ref.shape, jnp.int32)
    for user in range(out_ref.shape[0]):
        owner = lax.div(slot_ref[user], local) ^ lax.axis_index("cand")
        want = jnp.where(row == user, owner, want)
    out_ref[...] = want


def choose_pool(
    half, ids_ref, pool_ref, _, model_ref, cand_ref
):
    users, rows = ids_ref.shape
    numbers = lax.broadcasted_iota(jnp.int32, (pool_ref.shape[0], rows), 0)
    for axis, out_ref in (("mp", model_ref), ("cand", cand_ref)):
        width = out_ref.shape[1]
        cols = aligned(lax.axis_index(axis) % (half // width), width)
        for user in range(users):
            chosen = (numbers == ids_ref[pl.ds(user, 1), :]).astype(BF16)
            out_ref[pl.ds(user * rows, rows), :] = lax.dot_general(
                chosen, pool_ref[:, cols], (((0,), (0,)), ((), ())), preferred_element_type=F32
            ).astype(BF16)


def tiles(width, step=512):
    step = min(step, width)
    return [pl.ds(i, step) for i in range(0, width, step)]


def multiply(rows_ref, weight_ref, out_ref, scale_ref=None):
    for cols in tiles(out_ref.shape[1]):
        value = jnp.dot(rows_ref[...], weight_ref[:, cols], preferred_element_type=F32)
        out_ref[:, cols] = value if scale_ref is None else scale_ref[:, cols].astype(F32) * value


def pool_terms(half, rows_ref, weight_ref, keep_ref, send_ref, terms_ref):
    inside = lax.axis_index("mp") < half // rows_ref.shape[1]

    @pl.when(inside)
    def _():
        keep_ref[...] = jnp.zeros_like(keep_ref)
        send_ref[...] = jnp.zeros_like(send_ref)

    @pl.when(jnp.logical_not(inside))
    def _():
        multiply(rows_ref, weight_ref, terms_ref)
        low = lax.axis_index("mp") % 2
        size = keep_ref.shape[0]
        keep_ref[...] = terms_ref[aligned(low, size), :]
        send_ref[...] = terms_ref[aligned(1 - low, size), :].astype(BF16)


def user_terms(
    half, want_ref, weight_ref, pool_model_ref, pool_cand_ref, *refs
):
    *part_refs, model_ref, cand_ref, terms_ref = refs
    users = part_refs[0].shape[0]
    terms_ref[...] = jnp.zeros_like(terms_ref)
    for axis, pool_ref, out_ref in (
        ("mp", pool_model_ref, model_ref),
        ("cand", pool_cand_ref, cand_ref),
    ):
        rows, width = out_ref.shape
        block = lax.axis_index(axis)
        inside = block < half // width

        @pl.when(inside)
        def _():
            cols = aligned(block % (half // width), width)
            parts = [part_ref[:, cols] for part_ref in part_refs]
            chosen = parts[0].astype(F32)
            want = jnp.broadcast_to(want_ref[:, :1], chosen.shape)
            for bit in range(1, len(parts)):
                chosen = jnp.where(want == bit, parts[bit].astype(F32), chosen)
            for user in range(users):
                out_ref[pl.ds(user * (rows // users), rows // users), :] = jnp.broadcast_to(
                    chosen[user : user + 1], (rows // users, width)
                ).astype(BF16)
            if axis == "mp":
                padded = chosen
                if users < 8:
                    padded = jnp.concatenate([chosen, jnp.zeros((8 - users, width), F32)], axis=0)
                padded = padded.astype(BF16)
                for tile in tiles(terms_ref.shape[1]):
                    value = jnp.dot(padded, weight_ref[:, tile], preferred_element_type=F32)
                    terms_ref[:, tile] = value[:users]

        @pl.when(jnp.logical_not(inside))
        def _():
            out_ref[...] = pool_ref[...]


def add_up(keep_ref, other_ref, sum_ref, send_ref):
    total = keep_ref[...] + other_ref[...].astype(F32)
    sum_ref[...] = total
    send_ref[...] = total.astype(BF16)


def add_own_columns(terms_ref, rows_ref, have, want):
    width, wanted = rows_ref.shape[1], terms_ref.shape[1]
    small = min(width, wanted)
    ratio = max(width, wanted) // small
    assert max(width, wanted) == ratio * small
    if width >= wanted:
        inside, here, there = want // ratio == have, aligned(want % ratio, small), slice(None)
    else:
        inside, here, there = have // ratio == want, slice(None), aligned(have % ratio, small)

    @pl.when(inside)
    def _():
        terms_ref[:, there] += rows_ref[:, here].astype(F32)


def layer_two(
    mine_ref, other_ref, user_ref, user_other_ref, bias_ref, cand_ref, base_ref, weight_ref, *refs
):
    *out_refs, rows_ref, terms_ref, user_sum_ref = refs
    low = lax.axis_index("mp") % 2
    size = mine_ref.shape[0]
    users = user_ref.shape[0]
    assert users == 1 or users % 2 == 0
    user_sum_ref[...] = user_ref[...] + user_other_ref[...] + bias_ref[...]
    each = max(users // 2, 1)
    for index, pool_ref in ((low, mine_ref), (1 - low, other_ref)):
        for piece in range(each):
            user = index * each + piece if users > 1 else 0
            part = pl.ds(piece * (size // each), size // each)
            here = aligned(index * each + piece, size // each)
            base = cand_ref[here, :].astype(F32)
            total = pool_ref[part, :].astype(F32) + user_sum_ref[pl.ds(user, 1), :]
            rows_ref[here, :] = (base * total + base).astype(BF16)
    multiply(rows_ref, weight_ref, terms_ref, base_ref)
    cand = lax.axis_index("cand")
    add_own_columns(terms_ref, rows_ref, cand, lax.axis_index("mp"))
    if len(out_refs) == 1:
        out_refs[0][...] = terms_ref[...].astype(BF16)
        return
    for bit, out_ref in enumerate(out_refs):
        out_ref[...] = terms_ref[aligned(cand ^ bit, out_ref.shape[0]), :].astype(out_ref.dtype)


def cross_rows(base_ref, bias_ref, *refs):
    *part_refs, out_ref = refs
    total = part_refs[0][...].astype(F32)
    for part_ref in part_refs[1:]:
        total = total + part_ref[...].astype(F32)
    base = base_ref[aligned(lax.axis_index("cand"), out_ref.shape[0]), :].astype(F32)
    out_ref[...] = (total + base * bias_ref[...]).astype(BF16)


def split_low(axis_bit, terms_ref, keep_ref, send_ref, size):
    for pair in range(keep_ref.shape[0] // size):
        rows = pl.ds(pair * size, size)
        keep_ref[rows, :] = terms_ref[aligned(2 * pair + axis_bit, size), :]
        send_ref[rows, :] = terms_ref[aligned(2 * pair + 1 - axis_bit, size), :].astype(BF16)


def score_map(base_ref, score_ref, weight_ref, out_ref, rows_ref, score_row_ref):
    rows_ref[...] = (base_ref[...].astype(F32) * score_ref[...].astype(F32)).astype(BF16)
    for part in tiles(out_ref.shape[1]):
        out_ref[:, part] = lax.dot_general(
            rows_ref[...], weight_ref[part, :], (((1,), (1,)), ((), ())), preferred_element_type=F32
        )
    score_row_ref[...] = jnp.broadcast_to(score_ref[...].astype(F32), score_row_ref.shape)
    add_own_columns(out_ref, score_row_ref, lax.axis_index("cand"), lax.axis_index("mp"))


def score_rows(map_ref, base_ref, bias_ref, score_ref, *refs):
    *part_refs, rows_ref, logit_ref = refs
    cand = lax.axis_index("cand")
    if len(part_refs) == 1:
        rows_ref[...] = part_refs[0][...]
    else:
        for bit, part_ref in enumerate(part_refs):
            rows_ref[aligned(cand ^ bit, part_ref.shape[0]), :] = part_ref[...]
    once = (lax.axis_index("mp") == 0).astype(F32)
    blocks, size = logit_ref.shape
    lanes = 128
    for block in range(blocks):
        rows = pl.ds(block * size, size)
        total = jnp.zeros((size, lanes), F32)
        for start in range(0, map_ref.shape[1], lanes):
            cols = pl.ds(start, lanes)
            total = total + rows_ref[rows, cols].astype(F32) * map_ref[rows, cols]
        for start in range(0, base_ref.shape[1], lanes):
            cols = pl.ds(start, lanes)
            weight = bias_ref[:, cols] * score_ref[:, cols].astype(F32) * once
            total = total + base_ref[rows, cols].astype(F32) * weight
        logit_ref[pl.ds(block, 1), :] = jnp.sum(total.T, axis=0, keepdims=True)


def layer_three(row_block, base_ref, weight_ref, rows_ref, keep_ref, send_ref, terms_ref):
    multiply(rows_ref, weight_ref, terms_ref, base_ref)
    model = lax.axis_index("mp")
    add_own_columns(terms_ref, rows_ref, model, lax.axis_index("cand"))
    split_low(model % 2, terms_ref, keep_ref, send_ref, row_block)


def halve(row_block, bit, keep_ref, other_ref, kept_ref, send_ref, terms_ref):
    terms_ref[...] = keep_ref[...] + other_ref[...].astype(F32)
    split_low((lax.axis_index("mp") // bit) % 2, terms_ref, kept_ref, send_ref, row_block)


def finish(keep_ref, other_ref, base_ref, bias_ref, *refs):
    *part_refs, out_ref, logit_ref, sum_ref = refs
    model = lax.axis_index("mp")
    base = base_ref[aligned(model, out_ref.shape[0]), :].astype(F32)
    cross = keep_ref[...] + other_ref[...].astype(F32) + base * bias_ref[...]
    out_ref[...] = cross.astype(BF16)
    total = part_refs[0][...]
    for part_ref in part_refs[1:]:
        total = total + part_ref[...]
    sum_ref[...] = total
    logit_ref[...] = sum_ref[pl.ds(model, 1), :]


def body(
    user_feats,
    user_slot,
    cand_pool,
    cand_ids,
    first_weight,
    first_bias,
    second_weight,
    second_bias,
    third_weight,
    third_bias,
    score_weight,
):
    cand_count = lax.axis_size("cand")
    model_count = lax.axis_size("mp")
    local, half_width = user_feats.shape
    full_width = 2 * half_width
    user_count, per_user = cand_ids.shape
    row_total = user_count * per_user
    col_block = full_width // cand_count
    feat_block = full_width // model_count
    local_rows = row_total // cand_count
    row_block = row_total // model_count
    half_rows = row_total // 2
    flops = 2 * row_total * col_block * feat_block
    direct = cand_count <= DIRECT

    if local > 1:
        user_feats = jnp.take(user_feats, user_slot % local, axis=0)
    elif user_count > 1:
        user_feats = jnp.broadcast_to(user_feats, (user_count, half_width))
    (staged,) = call(stage, [((8, 128), F32)], [], flops=STAGE_FLOPS)
    users = user_feats
    pool_model, pool_cand = call(
        functools.partial(choose_pool, half_width),
        [
            ((row_total, feat_block), BF16),
            ((row_total, col_block), BF16),
        ],
        [cand_ids, cand_pool, staged],
        limit=8 * MIB,
    )
    (want,) = call(
        functools.partial(owner_steps, local),
        [((user_count, 128), jnp.int32)],
        [user_slot],
        smem=(0,),
    )
    if direct:
        users = [users] + [swap(users, "cand", bit) for bit in range(1, cand_count)]
    else:
        slots = user_slot.reshape(-1, 1)
        for bit in bits_of(cand_count):
            (users,) = call(
                functools.partial(choose_user, local, bit),
                [((user_count, half_width), BF16)],
                [slots, users, swap(users, "cand", bit)],
            )
        users = [users]

    half_outs = [((half_rows, col_block), F32), ((half_rows, col_block), BF16)]
    keep, send = call(
        functools.partial(pool_terms, half_width),
        half_outs,
        [pool_model, first_weight],
        scratch=[pltpu.VMEM((row_total, col_block), F32)],
        flops=flops,
        limit=12 * MIB,
    )
    for bit in bits_of(model_count):
        keep, send = call(add_up, half_outs, [keep, swap(send, "mp", bit)])
    pool_other = swap(send, "mp", 1)

    base_model, base_cand, user_sum = call(
        functools.partial(user_terms, half_width),
        [
            ((row_total, feat_block), BF16),
            ((row_total, col_block), BF16),
            ((user_count, col_block), F32),
        ],
        [want, first_weight, pool_model, pool_cand, *users],
        flops=flops,
        limit=12 * MIB,
    )
    *bits, last_bit = bits_of(model_count)
    for bit in bits:
        other = swap(user_sum, "mp", bit)
        (user_sum,) = call(add_to, [((user_count, col_block), F32)], [user_sum, other])
    user_other = swap(user_sum, "mp", last_bit)

    if direct:
        outs = [((local_rows, feat_block), BF16 if bit else F32) for bit in range(cand_count)]
    else:
        outs = [((row_total, feat_block), BF16)]
    parts = call(
        layer_two,
        outs,
        [
            keep, pool_other, user_sum, user_other, first_bias.reshape(1, -1), base_cand,
            base_model, second_weight,
        ],
        scratch=[
            pltpu.VMEM((row_total, col_block), BF16),
            pltpu.VMEM((row_total, feat_block), F32),
            pltpu.VMEM((user_count, col_block), F32),
        ],
        flops=flops,
        limit=12 * MIB,
    )
    if direct:
        parts = [parts[0]] + [swap(parts[bit], "cand", bit) for bit in range(1, cand_count)]
    else:
        parts = [lax.psum_scatter(parts[0], "cand", scatter_dimension=0, tiled=True)]
    score = score_weight.reshape(1, -1)
    (mapped,) = call(
        score_map,
        [((row_total, feat_block), F32)],
        [base_cand, score, third_weight],
        scratch=[pltpu.VMEM((row_total, col_block), BF16), pltpu.VMEM((row_total, col_block), F32)],
        flops=flops,
        limit=12 * MIB,
    )
    (block,) = call(
        cross_rows,
        [((local_rows, feat_block), BF16)],
        [base_model, second_bias.reshape(1, -1), *parts],
    )
    if direct:
        parts = [block] + [swap(block, "cand", bit) for bit in range(1, cand_count)]
    else:
        parts = [lax.all_gather(block, "cand", axis=0, tiled=True)]

    bias = third_bias.reshape(1, -1)
    logit_out = [((model_count, row_block), F32)]
    cross_two, logits = call(
        score_rows,
        [((row_total, feat_block), BF16)] + logit_out,
        [mapped, base_cand, bias, score, *parts],
    )
    rows = row_total // 2
    keep, send = call(
        functools.partial(layer_three, row_block),
        [((rows, col_block), F32), ((rows, col_block), BF16)],
        [base_cand, third_weight, cross_two],
        scratch=[pltpu.VMEM((row_total, col_block), F32)],
        flops=flops,
        limit=12 * MIB,
    )
    other = swap(send, "mp", 1)
    for bit in bits_of(model_count)[1:]:
        scratch = [pltpu.VMEM((rows, col_block), F32)]
        rows //= 2
        keep, send = call(
            functools.partial(halve, row_block, bit),
            [((rows, col_block), F32), ((rows, col_block), BF16)],
            [keep, other],
            scratch=scratch,
        )
        other = swap(send, "mp", bit)

    for bit in bits_of(model_count):
        (logits,) = call(add_to, logit_out, [logits, swap(logits, "mp", bit)])
    if direct:
        parts = [logits]
        parts += [swap(logits, "cand", bit) for bit in range(1, cand_count)]
    else:
        for bit in bits_of(cand_count):
            (logits,) = call(add_to, logit_out, [logits, swap(logits, "cand", bit)])
        parts = [logits]
    crossed, logits = call(
        finish,
        [((row_block, col_block), BF16), ((1, row_block), F32)],
        [keep, other, base_cand, bias, *parts],
        scratch=[pltpu.VMEM((model_count, row_block), F32)],
    )
    return (crossed, logits.reshape(-1))


def solution(mesh):
    in_specs = (
        P(("groups", "cand"), None),
        P("groups"),
        P("groups", None),
        P("groups", None),
        P("mp", "cand"),
        P("cand"),
        P("cand", "mp"),
        P("mp"),
        P("mp", "cand"),
        P("cand"),
        P("cand"),
    )
    out_specs = (P(("groups", "mp"), "cand"), P(("groups", "mp")))

    return jax.shard_map(body, mesh=mesh, in_specs=in_specs, out_specs=out_specs, check_vma=False)
```

```python
import functools

import jax
import jax.numpy as jnp
from jax import lax
from jax.experimental import pallas as pl
from jax.experimental.pallas import tpu as pltpu
from jax.sharding import PartitionSpec as P


F32 = jnp.float32
BF16 = jnp.bfloat16
LANES = 128
DIRECT = 4
MIB = 1024 * 1024
STAGE_FLOPS = 1 << 34


def bits_of(count):
    bits, bit = [], 1
    while bit < count:
        bits.append(bit)
        bit *= 2
    assert bit == count
    return bits


def swap(value, axis, bit):
    count = lax.axis_size(axis)
    return lax.ppermute(value, axis, [(i, i ^ bit) for i in range(count)])


def call(kernel, outs, args, scratch=(), hbm=(), smem=(), flops=0, limit=6 * MIB):
    moved = sum(a.size * a.dtype.itemsize for a in args if a.size < 2 * MIB)
    moved += sum(functools.reduce(lambda a, b: a * b, s) * jnp.dtype(d).itemsize for s, d in outs)
    return pl.pallas_call(
        kernel,
        out_shape=[jax.ShapeDtypeStruct(s, d) for s, d in outs],
        in_specs=[
            pl.BlockSpec(
                memory_space=pltpu.HBM if i in hbm else pltpu.SMEM if i in smem else pltpu.VMEM
            )
            for i in range(len(args))
        ],
        out_specs=[pl.BlockSpec(memory_space=pltpu.VMEM)] * len(outs),
        scratch_shapes=list(scratch),
        compiler_params=pltpu.CompilerParams(vmem_limit_bytes=limit),
        cost_estimate=pl.CostEstimate(flops=flops, bytes_accessed=moved, transcendentals=0),
    )(*[pltpu.with_memory_space_constraint(a, pltpu.HBM) if i in hbm else a for i, a in enumerate(args)])


def aligned(index, size):
    return pl.ds(pl.multiple_of(index * size, size), size)


def add_to(*refs):
    *part_refs, out_ref = refs
    total = part_refs[0][...]
    for part_ref in part_refs[1:]:
        total = total + part_ref[...]
    out_ref[...] = total


def stage(out_ref):
    out_ref[...] = jnp.zeros_like(out_ref)


def choose_user(local, bit, slot_ref, own_ref, other_ref, out_ref):
    want = (slot_ref[...] // local) ^ lax.axis_index("cand")
    other, own = other_ref[...].astype(F32), own_ref[...].astype(F32)
    out_ref[...] = jnp.where((jnp.broadcast_to(want, own.shape) & bit) != 0, other, own).astype(BF16)


def owner_steps(local, slot_ref, out_ref):
    row = lax.broadcasted_iota(jnp.int32, out_ref.shape, 0)
    want = jnp.zeros(out_ref.shape, jnp.int32)
    for user in range(out_ref.shape[0]):
        owner = lax.div(slot_ref[user], local) ^ lax.axis_index("cand")
        want = jnp.where(row == user, owner, want)
    out_ref[...] = want


def choose_pool(
    half, ids_ref, pool_ref, _, model_ref, cand_ref
):
    users, rows = ids_ref.shape
    numbers = lax.broadcasted_iota(jnp.int32, (pool_ref.shape[0], rows), 0)
    for axis, out_ref in (("mp", model_ref), ("cand", cand_ref)):
        width = out_ref.shape[1]
        cols = aligned(lax.axis_index(axis) % (half // width), width)
        for user in range(users):
            chosen = (numbers == ids_ref[pl.ds(user, 1), :]).astype(BF16)
            out_ref[pl.ds(user * rows, rows), :] = lax.dot_general(
                chosen, pool_ref[:, cols], (((0,), (0,)), ((), ())), preferred_element_type=F32
            ).astype(BF16)


def tiles(width, step=512):
    step = min(step, width)
    return [pl.ds(i, step) for i in range(0, width, step)]


def multiply(rows_ref, weight_ref, out_ref, scale_ref=None):
    for cols in tiles(out_ref.shape[1]):
        value = jnp.dot(rows_ref[...], weight_ref[:, cols], preferred_element_type=F32)
        out_ref[:, cols] = value if scale_ref is None else scale_ref[:, cols].astype(F32) * value


def pool_terms(half, rows_ref, weight_ref, keep_ref, send_ref, terms_ref):
    inside = lax.axis_index("mp") < half // rows_ref.shape[1]

    @pl.when(inside)
    def _():
        keep_ref[...] = jnp.zeros_like(keep_ref)
        send_ref[...] = jnp.zeros_like(send_ref)

    @pl.when(jnp.logical_not(inside))
    def _():
        multiply(rows_ref, weight_ref, terms_ref)
        low = lax.axis_index("mp") % 2
        size = keep_ref.shape[0]
        keep_ref[...] = terms_ref[aligned(low, size), :]
        send_ref[...] = terms_ref[aligned(1 - low, size), :].astype(BF16)


def user_terms(
    half, want_ref, weight_ref, pool_model_ref, pool_cand_ref, *refs
):
    *part_refs, model_ref, cand_ref, terms_ref = refs
    users = part_refs[0].shape[0]
    terms_ref[...] = jnp.zeros_like(terms_ref)
    for axis, pool_ref, out_ref in (
        ("mp", pool_model_ref, model_ref),
        ("cand", pool_cand_ref, cand_ref),
    ):
        rows, width = out_ref.shape
        block = lax.axis_index(axis)
        inside = block < half // width

        @pl.when(inside)
        def _():
            cols = aligned(block % (half // width), width)
            parts = [part_ref[:, cols] for part_ref in part_refs]
            chosen = parts[0].astype(F32)
            want = jnp.broadcast_to(want_ref[:, :1], chosen.shape)
            for bit in range(1, len(parts)):
                chosen = jnp.where(want == bit, parts[bit].astype(F32), chosen)
            for user in range(users):
                out_ref[pl.ds(user * (rows // users), rows // users), :] = jnp.broadcast_to(
                    chosen[user : user + 1], (rows // users, width)
                ).astype(BF16)
            if axis == "mp":
                padded = chosen
                if users < 8:
                    padded = jnp.concatenate([chosen, jnp.zeros((8 - users, width), F32)], axis=0)
                padded = padded.astype(BF16)
                for tile in tiles(terms_ref.shape[1]):
                    value = jnp.dot(padded, weight_ref[:, tile], preferred_element_type=F32)
                    terms_ref[:, tile] = value[:users]

        @pl.when(jnp.logical_not(inside))
        def _():
            out_ref[...] = pool_ref[...]


def add_up(keep_ref, other_ref, sum_ref, send_ref):
    total = keep_ref[...] + other_ref[...].astype(F32)
    sum_ref[...] = total
    send_ref[...] = total.astype(BF16)


def add_own_columns(terms_ref, rows_ref, have, want):
    width, wanted = rows_ref.shape[1], terms_ref.shape[1]
    small = min(width, wanted)
    ratio = max(width, wanted) // small
    assert max(width, wanted) == ratio * small
    if width >= wanted:
        inside, here, there = want // ratio == have, aligned(want % ratio, small), slice(None)
    else:
        inside, here, there = have // ratio == want, slice(None), aligned(have % ratio, small)

    @pl.when(inside)
    def _():
        terms_ref[:, there] += rows_ref[:, here].astype(F32)


def layer_two(
    mine_ref, other_ref, user_ref, user_other_ref, bias_ref, cand_ref, base_ref, weight_ref, *refs
):
    *out_refs, rows_ref, terms_ref, user_sum_ref = refs
    low = lax.axis_index("mp") % 2
    size = mine_ref.shape[0]
    users = user_ref.shape[0]
    assert users == 1 or users % 2 == 0
    user_sum_ref[...] = user_ref[...] + user_other_ref[...] + bias_ref[...]
    each = max(users // 2, 1)
    for index, pool_ref in ((low, mine_ref), (1 - low, other_ref)):
        for piece in range(each):
            user = index * each + piece if users > 1 else 0
            part = pl.ds(piece * (size // each), size // each)
            here = aligned(index * each + piece, size // each)
            base = cand_ref[here, :].astype(F32)
            total = pool_ref[part, :].astype(F32) + user_sum_ref[pl.ds(user, 1), :]
            rows_ref[here, :] = (base * total + base).astype(BF16)
    multiply(rows_ref, weight_ref, terms_ref, base_ref)
    cand = lax.axis_index("cand")
    add_own_columns(terms_ref, rows_ref, cand, lax.axis_index("mp"))
    if len(out_refs) == 1:
        out_refs[0][...] = terms_ref[...].astype(BF16)
        return
    for bit, out_ref in enumerate(out_refs):
        out_ref[...] = terms_ref[aligned(cand ^ bit, out_ref.shape[0]), :].astype(out_ref.dtype)


def cross_rows(base_ref, bias_ref, *refs):
    *part_refs, out_ref = refs
    total = part_refs[0][...].astype(F32)
    for part_ref in part_refs[1:]:
        total = total + part_ref[...].astype(F32)
    base = base_ref[aligned(lax.axis_index("cand"), out_ref.shape[0]), :].astype(F32)
    out_ref[...] = (total + base * bias_ref[...]).astype(BF16)


def score_map(half, users, base_ref, score_ref, bias_ref, weight_ref, *refs):
    *out_refs, rows_ref, map_ref, score_row_ref = refs
    rows, width = base_ref.shape
    columns = map_ref.shape[1]
    each = rows // users
    inside = lax.axis_index("cand") < half // width
    score = score_ref[...].astype(F32)

    def product(count):
        for part in tiles(columns):
            map_ref[pl.ds(0, count), part] = lax.dot_general(
                rows_ref[pl.ds(0, count), :],
                weight_ref[part, :],
                (((1,), (1,)), ((), ())),
                preferred_element_type=F32,
            )

    @pl.when(inside)
    def _():
        small = max(users, 16)
        score_row_ref[pl.ds(0, small), :] = jnp.zeros((small, width), F32)
        for user in range(users):
            base = base_ref[pl.ds(user * each, each), :].astype(F32)[:1]
            score_row_ref[pl.ds(user, 1), :] = base * score
        rows_ref[pl.ds(0, small), :] = score_row_ref[pl.ds(0, small), :].astype(BF16)
        product(small)
        for user in reversed(range(users)):
            row = map_ref[pl.ds(user, 1), :]
            map_ref[pl.ds(user * each, each), :] = jnp.broadcast_to(row, (each, columns))

    @pl.when(jnp.logical_not(inside))
    def _():
        rows_ref[...] = (base_ref[...].astype(F32) * score).astype(BF16)
        product(rows)

    score_row_ref[...] = jnp.broadcast_to(score, score_row_ref.shape)
    add_own_columns(map_ref, score_row_ref, lax.axis_index("cand"), lax.axis_index("mp"))
    weight = bias_ref[...] * score
    for bit, out_ref in enumerate(out_refs):
        size = out_ref.shape[0]
        block = aligned(lax.axis_index("cand") ^ bit, size)
        out_ref[:, pl.ds(0, columns)] = map_ref[block, :].astype(out_ref.dtype)
        total = jnp.zeros((size, LANES), F32)
        for start in range(0, width, LANES):
            cols = pl.ds(start, LANES)
            total = total + base_ref[block, cols].astype(F32) * weight[:, start : start + LANES]
        out_ref[:, pl.ds(columns, LANES)] = total.astype(out_ref.dtype)


def cross_scored(count, base_ref, bias_ref, *refs):
    part_refs, map_refs, (out_ref,) = refs[:count], refs[count : 2 * count], refs[2 * count :]
    size, width = part_refs[0].shape
    base = base_ref[aligned(lax.axis_index("cand"), size), :].astype(F32)
    once = (lax.axis_index("mp") == 0).astype(F32)

    def added(refs, cols):
        total = refs[0][:, cols].astype(F32)
        for ref in refs[1:]:
            total = total + ref[:, cols].astype(F32)
        return total

    score = added(map_refs, pl.ds(width, LANES)) * once
    for start in range(0, width, LANES):
        cols = pl.ds(start, LANES)
        cross = added(part_refs, cols) + base[:, start : start + LANES] * bias_ref[:, cols]
        rounded = cross.astype(BF16)
        out_ref[:, cols] = rounded
        score = score + rounded.astype(F32) * added(map_refs, cols)
    high = score.astype(BF16)
    out_ref[:, pl.ds(width, LANES)] = high
    out_ref[:, pl.ds(width + LANES, LANES)] = (score - high.astype(F32)).astype(BF16)


def assemble(*refs):
    *part_refs, rows_ref, logit_ref = refs
    width = rows_ref.shape[1]
    for bit, part_ref in enumerate(part_refs):
        block = lax.axis_index("cand") ^ bit
        rows_ref[aligned(block, part_ref.shape[0]), :] = part_ref[:, pl.ds(0, width)]
        lanes = part_ref[:, pl.ds(width, LANES)].astype(F32)
        lanes = lanes + part_ref[:, pl.ds(width + LANES, LANES)].astype(F32)
        logit_ref[pl.ds(block, 1), :] = jnp.sum(lanes.T, axis=0, keepdims=True)


def split_low(axis_bit, terms_ref, keep_ref, send_ref, size):
    for pair in range(keep_ref.shape[0] // size):
        rows = pl.ds(pair * size, size)
        keep_ref[rows, :] = terms_ref[aligned(2 * pair + axis_bit, size), :]
        send_ref[rows, :] = terms_ref[aligned(2 * pair + 1 - axis_bit, size), :].astype(BF16)


def layer_three(row_block, base_ref, weight_ref, rows_ref, keep_ref, send_ref, terms_ref):
    multiply(rows_ref, weight_ref, terms_ref, base_ref)
    model = lax.axis_index("mp")
    add_own_columns(terms_ref, rows_ref, model, lax.axis_index("cand"))
    split_low(model % 2, terms_ref, keep_ref, send_ref, row_block)


def halve(row_block, bit, keep_ref, other_ref, kept_ref, send_ref, terms_ref):
    terms_ref[...] = keep_ref[...] + other_ref[...].astype(F32)
    split_low((lax.axis_index("mp") // bit) % 2, terms_ref, kept_ref, send_ref, row_block)


def finish(keep_ref, other_ref, base_ref, bias_ref, total_ref, part_ref, out_ref, logit_ref, sum_ref):
    model = lax.axis_index("mp")
    base = base_ref[aligned(model, out_ref.shape[0]), :].astype(F32)
    cross = keep_ref[...] + other_ref[...].astype(F32) + base * bias_ref[...]
    out_ref[...] = cross.astype(BF16)
    sum_ref[...] = total_ref[...] + part_ref[...]
    logit_ref[...] = sum_ref[pl.ds(model, 1), :]


def finish_scored(keep_ref, other_ref, base_ref, bias_ref, score_ref, out_ref, logit_ref):
    base = base_ref[aligned(lax.axis_index("mp"), out_ref.shape[0]), :].astype(F32)
    cross = keep_ref[...] + other_ref[...].astype(F32) + base * bias_ref[...]
    out_ref[...] = cross.astype(BF16)
    logit_ref[...] = jnp.sum(cross * score_ref[...].astype(F32), axis=1, keepdims=True)


def body(
    user_feats,
    user_slot,
    cand_pool,
    cand_ids,
    first_weight,
    first_bias,
    second_weight,
    second_bias,
    third_weight,
    third_bias,
    score_weight,
):
    cand_count = lax.axis_size("cand")
    model_count = lax.axis_size("mp")
    local, half_width = user_feats.shape
    full_width = 2 * half_width
    user_count, per_user = cand_ids.shape
    row_total = user_count * per_user
    col_block = full_width // cand_count
    feat_block = full_width // model_count
    local_rows = row_total // cand_count
    row_block = row_total // model_count
    half_rows = row_total // 2
    flops = 2 * row_total * col_block * feat_block
    direct = cand_count <= DIRECT and cand_count == model_count
    score, bias = score_weight.reshape(1, -1), third_bias.reshape(1, -1)

    if local > 1:
        user_feats = jnp.take(user_feats, user_slot % local, axis=0)
    elif user_count > 1:
        user_feats = jnp.broadcast_to(user_feats, (user_count, half_width))
    (staged,) = call(stage, [((8, 128), F32)], [], flops=STAGE_FLOPS)
    users = user_feats
    pool_model, pool_cand = call(
        functools.partial(choose_pool, half_width),
        [
            ((row_total, feat_block), BF16),
            ((row_total, col_block), BF16),
        ],
        [cand_ids, cand_pool, staged],
        limit=8 * MIB,
    )
    (want,) = call(
        functools.partial(owner_steps, local),
        [((user_count, 128), jnp.int32)],
        [user_slot],
        smem=(0,),
    )
    if direct:
        users = [users] + [swap(users, "cand", bit) for bit in range(1, cand_count)]
    else:
        slots = user_slot.reshape(-1, 1)
        for bit in bits_of(cand_count):
            (users,) = call(
                functools.partial(choose_user, local, bit),
                [((user_count, half_width), BF16)],
                [slots, users, swap(users, "cand", bit)],
            )
        users = [users]

    half_outs = [((half_rows, col_block), F32), ((half_rows, col_block), BF16)]
    keep, send = call(
        functools.partial(pool_terms, half_width),
        half_outs,
        [pool_model, first_weight],
        scratch=[pltpu.VMEM((row_total, col_block), F32)],
        flops=flops,
        limit=12 * MIB,
    )
    for bit in bits_of(model_count):
        keep, send = call(add_up, half_outs, [keep, swap(send, "mp", bit)])
    pool_other = swap(send, "mp", 1)

    base_model, base_cand, user_sum = call(
        functools.partial(user_terms, half_width),
        [
            ((row_total, feat_block), BF16),
            ((row_total, col_block), BF16),
            ((user_count, col_block), F32),
        ],
        [want, first_weight, pool_model, pool_cand, *users],
        flops=flops,
        limit=12 * MIB,
    )
    *bits, last_bit = bits_of(model_count)
    for bit in bits:
        other = swap(user_sum, "mp", bit)
        (user_sum,) = call(add_to, [((user_count, col_block), F32)], [user_sum, other])
    user_other = swap(user_sum, "mp", last_bit)

    if direct:
        outs = [
            ((local_rows, feat_block + LANES), BF16 if bit else F32) for bit in range(cand_count)
        ]
        maps = call(
            functools.partial(score_map, half_width, user_count),
            outs,
            [base_cand, score, bias, third_weight],
            scratch=[
                pltpu.VMEM((row_total, col_block), BF16),
                pltpu.VMEM((row_total, feat_block), F32),
                pltpu.VMEM((row_total, col_block), F32),
            ],
            flops=flops,
            limit=12 * MIB,
        )
        maps = [maps[0]] + [swap(maps[bit], "cand", bit) for bit in range(1, cand_count)]
        outs = [((local_rows, feat_block), BF16 if bit else F32) for bit in range(cand_count)]
    else:
        outs = [((row_total, feat_block), BF16)]
    parts = call(
        layer_two,
        outs,
        [
            keep, pool_other, user_sum, user_other, first_bias.reshape(1, -1), base_cand,
            base_model, second_weight,
        ],
        scratch=[
            pltpu.VMEM((row_total, col_block), BF16),
            pltpu.VMEM((row_total, feat_block), F32),
            pltpu.VMEM((user_count, col_block), F32),
        ],
        flops=flops,
        limit=12 * MIB,
    )
    if direct:
        parts = [parts[0]] + [swap(parts[bit], "cand", bit) for bit in range(1, cand_count)]
    else:
        parts = [lax.psum_scatter(parts[0], "cand", scatter_dimension=0, tiled=True)]
    bias_two = second_bias.reshape(1, -1)
    if direct:
        (block,) = call(
            functools.partial(cross_scored, cand_count),
            [((local_rows, feat_block + 2 * LANES), BF16)],
            [base_model, bias_two, *parts, *maps],
        )
        parts = [block] + [swap(block, "cand", bit) for bit in range(1, cand_count)]
        logit_out = [((cand_count, local_rows), F32)]
        cross_two, logits = call(assemble, [((row_total, feat_block), BF16)] + logit_out, parts)
    else:
        (block,) = call(
            cross_rows, [((local_rows, feat_block), BF16)], [base_model, bias_two, *parts]
        )
        cross_two = lax.all_gather(block, "cand", axis=0, tiled=True)
    rows = row_total // 2
    keep, send = call(
        functools.partial(layer_three, row_block),
        [((rows, col_block), F32), ((rows, col_block), BF16)],
        [base_cand, third_weight, cross_two],
        scratch=[pltpu.VMEM((row_total, col_block), F32)],
        flops=flops,
        limit=12 * MIB,
    )
    other = swap(send, "mp", 1)
    for bit in bits_of(model_count)[1:]:
        scratch = [pltpu.VMEM((rows, col_block), F32)]
        rows //= 2
        keep, send = call(
            functools.partial(halve, row_block, bit),
            [((rows, col_block), F32), ((rows, col_block), BF16)],
            [keep, other],
            scratch=scratch,
        )
        other = swap(send, "mp", bit)

    rows = [keep, other, base_cand, bias]
    crossed_out = ((row_block, col_block), BF16)
    if direct:
        for bit in bits:
            (logits,) = call(add_to, logit_out, [logits, swap(logits, "mp", bit)])
        crossed, logits = call(
            finish,
            [crossed_out, ((1, row_block), F32)],
            [*rows, logits, swap(logits, "mp", last_bit)],
            scratch=[pltpu.VMEM((cand_count, local_rows), F32)],
        )
    else:
        crossed, logits = call(finish_scored, [crossed_out, ((row_block, 1), F32)], [*rows, score])
        logits = lax.psum(logits, "cand")
    return (crossed, logits.reshape(-1))


def solution(mesh):
    in_specs = (
        P(("groups", "cand"), None),
        P("groups"),
        P("groups", None),
        P("groups", None),
        P("mp", "cand"),
        P("cand"),
        P("cand", "mp"),
        P("mp"),
        P("mp", "cand"),
        P("cand"),
        P("cand"),
    )
    out_specs = (P(("groups", "mp"), "cand"), P(("groups", "mp")))

    return jax.shard_map(body, mesh=mesh, in_specs=in_specs, out_specs=out_specs, check_vma=False)
```

```python
import functools

import jax
import jax.numpy as jnp
from jax import lax
from jax.experimental import pallas as pl
from jax.experimental.pallas import tpu as pltpu
from jax.sharding import PartitionSpec as P


F32 = jnp.float32
BF16 = jnp.bfloat16
LANES = 128
DIRECT = 4
MIB = 1024 * 1024
STAGE_FLOPS = 1 << 34


def bits_of(count):
    bits, bit = [], 1
    while bit < count:
        bits.append(bit)
        bit *= 2
    assert bit == count
    return bits


def swap(value, axis, bit):
    count = lax.axis_size(axis)
    return lax.ppermute(value, axis, [(i, i ^ bit) for i in range(count)])


def call(kernel, outs, args, scratch=(), hbm=(), smem=(), flops=0, limit=6 * MIB):
    moved = sum(a.size * a.dtype.itemsize for a in args if a.size < 2 * MIB)
    moved += sum(functools.reduce(lambda a, b: a * b, s) * jnp.dtype(d).itemsize for s, d in outs)
    return pl.pallas_call(
        kernel,
        out_shape=[jax.ShapeDtypeStruct(s, d) for s, d in outs],
        in_specs=[
            pl.BlockSpec(
                memory_space=pltpu.HBM if i in hbm else pltpu.SMEM if i in smem else pltpu.VMEM
            )
            for i in range(len(args))
        ],
        out_specs=[pl.BlockSpec(memory_space=pltpu.VMEM)] * len(outs),
        scratch_shapes=list(scratch),
        compiler_params=pltpu.CompilerParams(vmem_limit_bytes=limit),
        cost_estimate=pl.CostEstimate(flops=flops, bytes_accessed=moved, transcendentals=0),
    )(*[pltpu.with_memory_space_constraint(a, pltpu.HBM) if i in hbm else a for i, a in enumerate(args)])


def aligned(index, size):
    return pl.ds(pl.multiple_of(index * size, size), size)


def add_to(*refs):
    *part_refs, out_ref = refs
    total = part_refs[0][...]
    for part_ref in part_refs[1:]:
        total = total + part_ref[...]
    out_ref[...] = total


def stage(out_ref):
    out_ref[...] = jnp.zeros_like(out_ref)


def choose_user(local, bit, slot_ref, own_ref, other_ref, out_ref):
    want = (slot_ref[...] // local) ^ lax.axis_index("cand")
    other, own = other_ref[...].astype(F32), own_ref[...].astype(F32)
    out_ref[...] = jnp.where((jnp.broadcast_to(want, own.shape) & bit) != 0, other, own).astype(BF16)


def owner_steps(local, slot_ref, out_ref):
    row = lax.broadcasted_iota(jnp.int32, out_ref.shape, 0)
    want = jnp.zeros(out_ref.shape, jnp.int32)
    for user in range(out_ref.shape[0]):
        owner = lax.div(slot_ref[user], local) ^ lax.axis_index("cand")
        want = jnp.where(row == user, owner, want)
    out_ref[...] = want


def choose_pool(
    half, ids_ref, pool_ref, _, model_ref, cand_ref
):
    users, rows = ids_ref.shape
    numbers = lax.broadcasted_iota(jnp.int32, (pool_ref.shape[0], rows), 0)
    for axis, out_ref in (("mp", model_ref), ("cand", cand_ref)):
        width = out_ref.shape[1]
        cols = aligned(lax.axis_index(axis) % (half // width), width)
        for user in range(users):
            chosen = (numbers == ids_ref[pl.ds(user, 1), :]).astype(BF16)
            out_ref[pl.ds(user * rows, rows), :] = lax.dot_general(
                chosen, pool_ref[:, cols], (((0,), (0,)), ((), ())), preferred_element_type=F32
            ).astype(BF16)


def tiles(width, step=512):
    step = min(step, width)
    return [pl.ds(i, step) for i in range(0, width, step)]


def multiply(rows_ref, weight_ref, out_ref, scale_ref=None):
    for cols in tiles(out_ref.shape[1]):
        value = jnp.dot(rows_ref[...], weight_ref[:, cols], preferred_element_type=F32)
        out_ref[:, cols] = value if scale_ref is None else scale_ref[:, cols].astype(F32) * value


def pool_terms(half, rows_ref, weight_ref, keep_ref, send_ref, terms_ref):
    inside = lax.axis_index("mp") < half // rows_ref.shape[1]

    @pl.when(inside)
    def _():
        keep_ref[...] = jnp.zeros_like(keep_ref)
        send_ref[...] = jnp.zeros_like(send_ref)

    @pl.when(jnp.logical_not(inside))
    def _():
        multiply(rows_ref, weight_ref, terms_ref)
        low = lax.axis_index("mp") % 2
        size = keep_ref.shape[0]
        keep_ref[...] = terms_ref[aligned(low, size), :]
        send_ref[...] = terms_ref[aligned(1 - low, size), :].astype(BF16)


def user_terms(
    half, want_ref, weight_ref, pool_model_ref, pool_cand_ref, *refs
):
    *part_refs, model_ref, cand_ref, terms_ref = refs
    users = part_refs[0].shape[0]
    terms_ref[...] = jnp.zeros_like(terms_ref)
    for axis, pool_ref, out_ref in (
        ("mp", pool_model_ref, model_ref),
        ("cand", pool_cand_ref, cand_ref),
    ):
        rows, width = out_ref.shape
        block = lax.axis_index(axis)
        inside = block < half // width

        @pl.when(inside)
        def _():
            cols = aligned(block % (half // width), width)
            parts = [part_ref[:, cols] for part_ref in part_refs]
            chosen = parts[0].astype(F32)
            want = jnp.broadcast_to(want_ref[:, :1], chosen.shape)
            for bit in range(1, len(parts)):
                chosen = jnp.where(want == bit, parts[bit].astype(F32), chosen)
            for user in range(users):
                out_ref[pl.ds(user * (rows // users), rows // users), :] = jnp.broadcast_to(
                    chosen[user : user + 1], (rows // users, width)
                ).astype(BF16)
            if axis == "mp":
                padded = chosen
                if users < 8:
                    padded = jnp.concatenate([chosen, jnp.zeros((8 - users, width), F32)], axis=0)
                padded = padded.astype(BF16)
                for tile in tiles(terms_ref.shape[1]):
                    value = jnp.dot(padded, weight_ref[:, tile], preferred_element_type=F32)
                    terms_ref[:, tile] = value[:users]

        @pl.when(jnp.logical_not(inside))
        def _():
            out_ref[...] = pool_ref[...]


def add_up(keep_ref, other_ref, sum_ref, send_ref):
    total = keep_ref[...] + other_ref[...].astype(F32)
    sum_ref[...] = total
    send_ref[...] = total.astype(BF16)


def add_own_columns(terms_ref, rows_ref, have, want):
    width, wanted = rows_ref.shape[1], terms_ref.shape[1]
    small = min(width, wanted)
    ratio = max(width, wanted) // small
    assert max(width, wanted) == ratio * small
    if width >= wanted:
        inside, here, there = want // ratio == have, aligned(want % ratio, small), slice(None)
    else:
        inside, here, there = have // ratio == want, slice(None), aligned(have % ratio, small)

    @pl.when(inside)
    def _():
        terms_ref[:, there] += rows_ref[:, here].astype(F32)


def layer_two(
    mine_ref, other_ref, user_ref, user_other_ref, bias_ref, cand_ref, base_ref, weight_ref, *refs
):
    *out_refs, rows_ref, terms_ref, user_sum_ref = refs
    low = lax.axis_index("mp") % 2
    size = mine_ref.shape[0]
    users = user_ref.shape[0]
    assert users == 1 or users % 2 == 0
    user_sum_ref[...] = user_ref[...] + user_other_ref[...] + bias_ref[...]
    each = max(users // 2, 1)
    for index, pool_ref in ((low, mine_ref), (1 - low, other_ref)):
        for piece in range(each):
            user = index * each + piece if users > 1 else 0
            part = pl.ds(piece * (size // each), size // each)
            here = aligned(index * each + piece, size // each)
            base = cand_ref[here, :].astype(F32)
            total = pool_ref[part, :].astype(F32) + user_sum_ref[pl.ds(user, 1), :]
            rows_ref[here, :] = (base * total + base).astype(BF16)
    multiply(rows_ref, weight_ref, terms_ref, base_ref)
    cand = lax.axis_index("cand")
    add_own_columns(terms_ref, rows_ref, cand, lax.axis_index("mp"))
    if len(out_refs) == 1:
        out_refs[0][...] = terms_ref[...].astype(BF16)
        return
    for bit, out_ref in enumerate(out_refs):
        out_ref[...] = terms_ref[aligned(cand ^ bit, out_ref.shape[0]), :].astype(out_ref.dtype)


def cross_rows(base_ref, bias_ref, *refs):
    *part_refs, out_ref = refs
    total = part_refs[0][...].astype(F32)
    for part_ref in part_refs[1:]:
        total = total + part_ref[...].astype(F32)
    base = base_ref[aligned(lax.axis_index("cand"), out_ref.shape[0]), :].astype(F32)
    out_ref[...] = (total + base * bias_ref[...]).astype(BF16)


def score_map(half, users, base_ref, score_ref, bias_ref, weight_ref, *refs):
    *out_refs, rows_ref, map_ref, score_row_ref = refs
    rows, width = base_ref.shape
    columns = map_ref.shape[1]
    each = rows // users
    inside = lax.axis_index("cand") < half // width
    score = score_ref[...].astype(F32)

    def product(count):
        for part in tiles(columns):
            map_ref[pl.ds(0, count), part] = lax.dot_general(
                rows_ref[pl.ds(0, count), :],
                weight_ref[part, :],
                (((1,), (1,)), ((), ())),
                preferred_element_type=F32,
            )

    @pl.when(inside)
    def _():
        small = max(users, 16)
        score_row_ref[pl.ds(0, small), :] = jnp.zeros((small, width), F32)
        for user in range(users):
            base = base_ref[pl.ds(user * each, each), :].astype(F32)[:1]
            score_row_ref[pl.ds(user, 1), :] = base * score
        rows_ref[pl.ds(0, small), :] = score_row_ref[pl.ds(0, small), :].astype(BF16)
        product(small)
        for user in reversed(range(users)):
            row = map_ref[pl.ds(user, 1), :]
            map_ref[pl.ds(user * each, each), :] = jnp.broadcast_to(row, (each, columns))

    @pl.when(jnp.logical_not(inside))
    def _():
        rows_ref[...] = (base_ref[...].astype(F32) * score).astype(BF16)
        product(rows)

    score_row_ref[...] = jnp.broadcast_to(score, score_row_ref.shape)
    add_own_columns(map_ref, score_row_ref, lax.axis_index("cand"), lax.axis_index("mp"))
    weight = bias_ref[...] * score
    for bit, out_ref in enumerate(out_refs):
        size = out_ref.shape[0]
        block = aligned(lax.axis_index("cand") ^ bit, size)
        out_ref[:, pl.ds(0, columns)] = map_ref[block, :].astype(out_ref.dtype)
        total = jnp.zeros((size, LANES), F32)
        for start in range(0, width, LANES):
            cols = pl.ds(start, LANES)
            total = total + base_ref[block, cols].astype(F32) * weight[:, start : start + LANES]
        out_ref[:, pl.ds(columns, LANES)] = total.astype(out_ref.dtype)


def cross_scored(count, base_ref, bias_ref, *refs):
    part_refs, map_refs, (out_ref,) = refs[:count], refs[count : 2 * count], refs[2 * count :]
    size, width = part_refs[0].shape
    base = base_ref[aligned(lax.axis_index("cand"), size), :].astype(F32)
    once = (lax.axis_index("mp") == 0).astype(F32)

    def added(refs, cols):
        total = refs[0][:, cols].astype(F32)
        for ref in refs[1:]:
            total = total + ref[:, cols].astype(F32)
        return total

    score = added(map_refs, pl.ds(width, LANES)) * once
    for start in range(0, width, LANES):
        cols = pl.ds(start, LANES)
        cross = added(part_refs, cols) + base[:, start : start + LANES] * bias_ref[:, cols]
        rounded = cross.astype(BF16)
        out_ref[:, cols] = rounded
        score = score + rounded.astype(F32) * added(map_refs, cols)
    score = score[:, : LANES // 2] + score[:, LANES // 2 :]
    high = score.astype(BF16).astype(F32)
    both = jnp.concatenate([high, score - high], axis=1)
    out_ref[:, pl.ds(width, LANES)] = both.astype(BF16)


def assemble(*refs):
    *part_refs, rows_ref, logit_ref = refs
    width = rows_ref.shape[1]
    for bit, part_ref in enumerate(part_refs):
        block = lax.axis_index("cand") ^ bit
        rows_ref[aligned(block, part_ref.shape[0]), :] = part_ref[:, pl.ds(0, width)]
        lanes = part_ref[:, pl.ds(width, LANES)].astype(F32)
        logit_ref[pl.ds(block, 1), :] = jnp.sum(lanes.T, axis=0, keepdims=True)


def split_low(axis_bit, terms_ref, keep_ref, send_ref, size):
    for pair in range(keep_ref.shape[0] // size):
        rows = pl.ds(pair * size, size)
        keep_ref[rows, :] = terms_ref[aligned(2 * pair + axis_bit, size), :]
        send_ref[rows, :] = terms_ref[aligned(2 * pair + 1 - axis_bit, size), :].astype(BF16)


def layer_three(row_block, base_ref, weight_ref, rows_ref, keep_ref, send_ref, terms_ref):
    multiply(rows_ref, weight_ref, terms_ref, base_ref)
    model = lax.axis_index("mp")
    add_own_columns(terms_ref, rows_ref, model, lax.axis_index("cand"))
    split_low(model % 2, terms_ref, keep_ref, send_ref, row_block)


def halve(row_block, bit, keep_ref, other_ref, kept_ref, send_ref, terms_ref):
    terms_ref[...] = keep_ref[...] + other_ref[...].astype(F32)
    split_low((lax.axis_index("mp") // bit) % 2, terms_ref, kept_ref, send_ref, row_block)


def finish(keep_ref, other_ref, base_ref, bias_ref, total_ref, part_ref, out_ref, logit_ref, sum_ref):
    model = lax.axis_index("mp")
    base = base_ref[aligned(model, out_ref.shape[0]), :].astype(F32)
    cross = keep_ref[...] + other_ref[...].astype(F32) + base * bias_ref[...]
    out_ref[...] = cross.astype(BF16)
    sum_ref[...] = total_ref[...] + part_ref[...]
    logit_ref[...] = sum_ref[pl.ds(model, 1), :]


def finish_scored(keep_ref, other_ref, base_ref, bias_ref, score_ref, out_ref, logit_ref):
    base = base_ref[aligned(lax.axis_index("mp"), out_ref.shape[0]), :].astype(F32)
    cross = keep_ref[...] + other_ref[...].astype(F32) + base * bias_ref[...]
    out_ref[...] = cross.astype(BF16)
    logit_ref[...] = jnp.sum(cross * score_ref[...].astype(F32), axis=1, keepdims=True)


def body(
    user_feats,
    user_slot,
    cand_pool,
    cand_ids,
    first_weight,
    first_bias,
    second_weight,
    second_bias,
    third_weight,
    third_bias,
    score_weight,
):
    cand_count = lax.axis_size("cand")
    model_count = lax.axis_size("mp")
    local, half_width = user_feats.shape
    full_width = 2 * half_width
    user_count, per_user = cand_ids.shape
    row_total = user_count * per_user
    col_block = full_width // cand_count
    feat_block = full_width // model_count
    local_rows = row_total // cand_count
    row_block = row_total // model_count
    half_rows = row_total // 2
    flops = 2 * row_total * col_block * feat_block
    direct = cand_count <= DIRECT and cand_count == model_count
    score, bias = score_weight.reshape(1, -1), third_bias.reshape(1, -1)

    if local > 1:
        user_feats = jnp.take(user_feats, user_slot % local, axis=0)
    elif user_count > 1:
        user_feats = jnp.broadcast_to(user_feats, (user_count, half_width))
    (staged,) = call(stage, [((8, 128), F32)], [], flops=STAGE_FLOPS)
    users = user_feats
    pool_model, pool_cand = call(
        functools.partial(choose_pool, half_width),
        [
            ((row_total, feat_block), BF16),
            ((row_total, col_block), BF16),
        ],
        [cand_ids, cand_pool, staged],
        limit=8 * MIB,
    )
    (want,) = call(
        functools.partial(owner_steps, local),
        [((user_count, 128), jnp.int32)],
        [user_slot],
        smem=(0,),
    )
    if direct:
        users = [users] + [swap(users, "cand", bit) for bit in range(1, cand_count)]
    else:
        slots = user_slot.reshape(-1, 1)
        for bit in bits_of(cand_count):
            (users,) = call(
                functools.partial(choose_user, local, bit),
                [((user_count, half_width), BF16)],
                [slots, users, swap(users, "cand", bit)],
            )
        users = [users]

    half_outs = [((half_rows, col_block), F32), ((half_rows, col_block), BF16)]
    keep, send = call(
        functools.partial(pool_terms, half_width),
        half_outs,
        [pool_model, first_weight],
        scratch=[pltpu.VMEM((row_total, col_block), F32)],
        flops=flops,
        limit=12 * MIB,
    )
    for bit in bits_of(model_count):
        keep, send = call(add_up, half_outs, [keep, swap(send, "mp", bit)])
    pool_other = swap(send, "mp", 1)

    base_model, base_cand, user_sum = call(
        functools.partial(user_terms, half_width),
        [
            ((row_total, feat_block), BF16),
            ((row_total, col_block), BF16),
            ((user_count, col_block), F32),
        ],
        [want, first_weight, pool_model, pool_cand, *users],
        flops=flops,
        limit=12 * MIB,
    )
    *bits, last_bit = bits_of(model_count)
    for bit in bits:
        other = swap(user_sum, "mp", bit)
        (user_sum,) = call(add_to, [((user_count, col_block), F32)], [user_sum, other])
    user_other = swap(user_sum, "mp", last_bit)

    if direct:
        outs = [
            ((local_rows, feat_block + LANES), BF16 if bit else F32) for bit in range(cand_count)
        ]
        maps = call(
            functools.partial(score_map, half_width, user_count),
            outs,
            [base_cand, score, bias, third_weight],
            scratch=[
                pltpu.VMEM((row_total, col_block), BF16),
                pltpu.VMEM((row_total, feat_block), F32),
                pltpu.VMEM((row_total, col_block), F32),
            ],
            flops=flops,
            limit=12 * MIB,
        )
        maps = [maps[0]] + [swap(maps[bit], "cand", bit) for bit in range(1, cand_count)]
        outs = [((local_rows, feat_block), BF16 if bit else F32) for bit in range(cand_count)]
    else:
        outs = [((row_total, feat_block), BF16)]
    parts = call(
        layer_two,
        outs,
        [
            keep, pool_other, user_sum, user_other, first_bias.reshape(1, -1), base_cand,
            base_model, second_weight,
        ],
        scratch=[
            pltpu.VMEM((row_total, col_block), BF16),
            pltpu.VMEM((row_total, feat_block), F32),
            pltpu.VMEM((user_count, col_block), F32),
        ],
        flops=flops,
        limit=12 * MIB,
    )
    if direct:
        parts = [parts[0]] + [swap(parts[bit], "cand", bit) for bit in range(1, cand_count)]
    else:
        parts = [lax.psum_scatter(parts[0], "cand", scatter_dimension=0, tiled=True)]
    bias_two = second_bias.reshape(1, -1)
    if direct:
        (block,) = call(
            functools.partial(cross_scored, cand_count),
            [((local_rows, feat_block + LANES), BF16)],
            [base_model, bias_two, *parts, *maps],
        )
        parts = [block] + [swap(block, "cand", bit) for bit in range(1, cand_count)]
        logit_out = [((cand_count, local_rows), F32)]
        cross_two, logits = call(assemble, [((row_total, feat_block), BF16)] + logit_out, parts)
    else:
        (block,) = call(
            cross_rows, [((local_rows, feat_block), BF16)], [base_model, bias_two, *parts]
        )
        cross_two = lax.all_gather(block, "cand", axis=0, tiled=True)
    rows = row_total // 2
    keep, send = call(
        functools.partial(layer_three, row_block),
        [((rows, col_block), F32), ((rows, col_block), BF16)],
        [base_cand, third_weight, cross_two],
        scratch=[pltpu.VMEM((row_total, col_block), F32)],
        flops=flops,
        limit=12 * MIB,
    )
    other = swap(send, "mp", 1)
    for bit in bits_of(model_count)[1:]:
        scratch = [pltpu.VMEM((rows, col_block), F32)]
        rows //= 2
        keep, send = call(
            functools.partial(halve, row_block, bit),
            [((rows, col_block), F32), ((rows, col_block), BF16)],
            [keep, other],
            scratch=scratch,
        )
        other = swap(send, "mp", bit)

    rows = [keep, other, base_cand, bias]
    crossed_out = ((row_block, col_block), BF16)
    if direct:
        for bit in bits:
            (logits,) = call(add_to, logit_out, [logits, swap(logits, "mp", bit)])
        crossed, logits = call(
            finish,
            [crossed_out, ((1, row_block), F32)],
            [*rows, logits, swap(logits, "mp", last_bit)],
            scratch=[pltpu.VMEM((cand_count, local_rows), F32)],
        )
    else:
        crossed, logits = call(finish_scored, [crossed_out, ((row_block, 1), F32)], [*rows, score])
        logits = lax.psum(logits, "cand")
    return (crossed, logits.reshape(-1))


def solution(mesh):
    in_specs = (
        P(("groups", "cand"), None),
        P("groups"),
        P("groups", None),
        P("groups", None),
        P("mp", "cand"),
        P("cand"),
        P("cand", "mp"),
        P("mp"),
        P("mp", "cand"),
        P("cand"),
        P("cand"),
    )
    out_specs = (P(("groups", "mp"), "cand"), P(("groups", "mp")))

    return jax.shard_map(body, mesh=mesh, in_specs=in_specs, out_specs=out_specs, check_vma=False)
```

```python
import functools

import jax
import jax.numpy as jnp
from jax import lax
from jax.experimental import pallas as pl
from jax.experimental.pallas import tpu as pltpu
from jax.sharding import PartitionSpec as P


F32 = jnp.float32
BF16 = jnp.bfloat16
LANES = 128
DIRECT = 4
MIB = 1024 * 1024
STAGE_FLOPS = 1 << 34


def bits_of(count):
    bits, bit = [], 1
    while bit < count:
        bits.append(bit)
        bit *= 2
    assert bit == count
    return bits


def swap(value, axis, bit):
    count = lax.axis_size(axis)
    return lax.ppermute(value, axis, [(i, i ^ bit) for i in range(count)])


def call(kernel, outs, args, scratch=(), hbm=(), smem=(), flops=0, limit=6 * MIB):
    moved = sum(a.size * a.dtype.itemsize for a in args if a.size < 2 * MIB)
    moved += sum(functools.reduce(lambda a, b: a * b, s) * jnp.dtype(d).itemsize for s, d in outs)
    return pl.pallas_call(
        kernel,
        out_shape=[jax.ShapeDtypeStruct(s, d) for s, d in outs],
        in_specs=[
            pl.BlockSpec(
                memory_space=pltpu.HBM if i in hbm else pltpu.SMEM if i in smem else pltpu.VMEM
            )
            for i in range(len(args))
        ],
        out_specs=[pl.BlockSpec(memory_space=pltpu.VMEM)] * len(outs),
        scratch_shapes=list(scratch),
        compiler_params=pltpu.CompilerParams(vmem_limit_bytes=limit),
        cost_estimate=pl.CostEstimate(flops=flops, bytes_accessed=moved, transcendentals=0),
    )(*[pltpu.with_memory_space_constraint(a, pltpu.HBM) if i in hbm else a for i, a in enumerate(args)])


def aligned(index, size):
    return pl.ds(pl.multiple_of(index * size, size), size)


def add_to(*refs):
    *part_refs, out_ref = refs
    total = part_refs[0][...]
    for part_ref in part_refs[1:]:
        total = total + part_ref[...]
    out_ref[...] = total


def stage(out_ref):
    out_ref[...] = jnp.zeros_like(out_ref)


def from_owner(want_ref, bit, own, other):
    differs = (jnp.broadcast_to(want_ref[:, :1], own.shape) & bit) != 0
    return jnp.where(differs, other.astype(F32), own.astype(F32))


def pair_rows(own_ref, other_ref, out_ref):
    rows = [own_ref[...].astype(F32), other_ref[...].astype(F32)]
    out_ref[...] = jnp.concatenate(rows, axis=0).astype(BF16)


def choose_user(bit, want_ref, own_ref, other_ref, out_ref):
    out_ref[...] = from_owner(want_ref, bit, own_ref[...], other_ref[...]).astype(BF16)


def owner_steps(local, slot_ref, out_ref):
    row = lax.broadcasted_iota(jnp.int32, out_ref.shape, 0)
    want = jnp.zeros(out_ref.shape, jnp.int32)
    for user in range(out_ref.shape[0]):
        owner = lax.div(slot_ref[user], local) ^ lax.axis_index("cand")
        want = jnp.where(row == user, owner, want)
    out_ref[...] = want


def choose_pool(
    half, ids_ref, pool_ref, _, model_ref, cand_ref
):
    users, rows = ids_ref.shape
    numbers = lax.broadcasted_iota(jnp.int32, (pool_ref.shape[0], rows), 0)
    for axis, out_ref in (("mp", model_ref), ("cand", cand_ref)):
        width = out_ref.shape[1]
        cols = aligned(lax.axis_index(axis) % (half // width), width)
        for user in range(users):
            chosen = (numbers == ids_ref[pl.ds(user, 1), :]).astype(BF16)
            out_ref[pl.ds(user * rows, rows), :] = lax.dot_general(
                chosen, pool_ref[:, cols], (((0,), (0,)), ((), ())), preferred_element_type=F32
            ).astype(BF16)


def tiles(width, step=512):
    step = min(step, width)
    return [pl.ds(i, step) for i in range(0, width, step)]


def multiply(rows_ref, weight_ref, out_ref, scale_ref=None):
    for cols in tiles(out_ref.shape[1]):
        value = jnp.dot(rows_ref[...], weight_ref[:, cols], preferred_element_type=F32)
        out_ref[:, cols] = value if scale_ref is None else scale_ref[:, cols].astype(F32) * value


def pool_terms(half, rows_ref, weight_ref, keep_ref, send_ref, terms_ref):
    inside = lax.axis_index("mp") < half // rows_ref.shape[1]

    @pl.when(inside)
    def _():
        keep_ref[...] = jnp.zeros_like(keep_ref)
        send_ref[...] = jnp.zeros_like(send_ref)

    @pl.when(jnp.logical_not(inside))
    def _():
        multiply(rows_ref, weight_ref, terms_ref)
        low = lax.axis_index("mp") % 2
        size = keep_ref.shape[0]
        keep_ref[...] = terms_ref[aligned(low, size), :]
        send_ref[...] = terms_ref[aligned(1 - low, size), :].astype(BF16)


def user_terms(
    half, bit, want_ref, weight_ref, pool_model_ref, pool_cand_ref, own_ref, other_ref,
    model_ref, cand_ref, terms_ref,
):
    users = terms_ref.shape[0]
    terms_ref[...] = jnp.zeros_like(terms_ref)
    for axis, pool_ref, out_ref in (
        ("mp", pool_model_ref, model_ref),
        ("cand", pool_cand_ref, cand_ref),
    ):
        rows, width = out_ref.shape
        block = lax.axis_index(axis)
        inside = block < half // width

        @pl.when(inside)
        def _():
            cols = aligned(block % (half // width), width)
            if own_ref.shape[0] == users:
                chosen = from_owner(want_ref, bit, own_ref[:, cols], other_ref[:, cols])
            else:
                own, other = own_ref[:, cols].astype(F32), other_ref[:, cols].astype(F32)
                near = from_owner(want_ref, bit, own[:users], other[:users])
                far = from_owner(want_ref, bit, own[users:], other[users:])
                chosen = from_owner(want_ref, bit // 2, near, far)
            for user in range(users):
                out_ref[pl.ds(user * (rows // users), rows // users), :] = jnp.broadcast_to(
                    chosen[user : user + 1], (rows // users, width)
                ).astype(BF16)
            if axis == "mp":
                padded = chosen
                if users < 8:
                    padded = jnp.concatenate([chosen, jnp.zeros((8 - users, width), F32)], axis=0)
                padded = padded.astype(BF16)
                for tile in tiles(terms_ref.shape[1]):
                    value = jnp.dot(padded, weight_ref[:, tile], preferred_element_type=F32)
                    terms_ref[:, tile] = value[:users]

        @pl.when(jnp.logical_not(inside))
        def _():
            out_ref[...] = pool_ref[...]


def add_up(keep_ref, other_ref, sum_ref, send_ref):
    total = keep_ref[...] + other_ref[...].astype(F32)
    sum_ref[...] = total
    send_ref[...] = total.astype(BF16)


def add_own_columns(terms_ref, rows_ref, have, want):
    width, wanted = rows_ref.shape[1], terms_ref.shape[1]
    small = min(width, wanted)
    ratio = max(width, wanted) // small
    assert max(width, wanted) == ratio * small
    if width >= wanted:
        inside, here, there = want // ratio == have, aligned(want % ratio, small), slice(None)
    else:
        inside, here, there = have // ratio == want, slice(None), aligned(have % ratio, small)

    @pl.when(inside)
    def _():
        terms_ref[:, there] += rows_ref[:, here].astype(F32)


def layer_two(
    mine_ref, other_ref, user_ref, user_other_ref, bias_ref, cand_ref, base_ref, weight_ref, *refs
):
    *out_refs, rows_ref, terms_ref, user_sum_ref = refs
    low = lax.axis_index("mp") % 2
    size = mine_ref.shape[0]
    users = user_ref.shape[0]
    assert users == 1 or users % 2 == 0
    user_sum_ref[...] = user_ref[...] + user_other_ref[...] + bias_ref[...]
    each = max(users // 2, 1)
    for index, pool_ref in ((low, mine_ref), (1 - low, other_ref)):
        for piece in range(each):
            user = index * each + piece if users > 1 else 0
            part = pl.ds(piece * (size // each), size // each)
            here = aligned(index * each + piece, size // each)
            base = cand_ref[here, :].astype(F32)
            total = pool_ref[part, :].astype(F32) + user_sum_ref[pl.ds(user, 1), :]
            rows_ref[here, :] = (base * total + base).astype(BF16)
    multiply(rows_ref, weight_ref, terms_ref, base_ref)
    cand = lax.axis_index("cand")
    add_own_columns(terms_ref, rows_ref, cand, lax.axis_index("mp"))
    if len(out_refs) == 1:
        out_refs[0][...] = terms_ref[...].astype(BF16)
        return
    for bit, out_ref in enumerate(out_refs):
        out_ref[...] = terms_ref[aligned(cand ^ bit, out_ref.shape[0]), :].astype(out_ref.dtype)


def cross_rows(base_ref, bias_ref, *refs):
    *part_refs, out_ref = refs
    total = part_refs[0][...].astype(F32)
    for part_ref in part_refs[1:]:
        total = total + part_ref[...].astype(F32)
    base = base_ref[aligned(lax.axis_index("cand"), out_ref.shape[0]), :].astype(F32)
    out_ref[...] = (total + base * bias_ref[...]).astype(BF16)


def score_map(half, users, base_ref, score_ref, bias_ref, weight_ref, *refs):
    *out_refs, rows_ref, map_ref, score_row_ref = refs
    rows, width = base_ref.shape
    columns = map_ref.shape[1]
    each = rows // users
    inside = lax.axis_index("cand") < half // width
    score = score_ref[...].astype(F32)

    def product(count):
        for part in tiles(columns):
            map_ref[pl.ds(0, count), part] = lax.dot_general(
                rows_ref[pl.ds(0, count), :],
                weight_ref[part, :],
                (((1,), (1,)), ((), ())),
                preferred_element_type=F32,
            )

    @pl.when(inside)
    def _():
        small = max(users, 16)
        score_row_ref[pl.ds(0, small), :] = jnp.zeros((small, width), F32)
        for user in range(users):
            base = base_ref[pl.ds(user * each, each), :].astype(F32)[:1]
            score_row_ref[pl.ds(user, 1), :] = base * score
        rows_ref[pl.ds(0, small), :] = score_row_ref[pl.ds(0, small), :].astype(BF16)
        product(small)
        for user in reversed(range(users)):
            row = map_ref[pl.ds(user, 1), :]
            map_ref[pl.ds(user * each, each), :] = jnp.broadcast_to(row, (each, columns))

    @pl.when(jnp.logical_not(inside))
    def _():
        rows_ref[...] = (base_ref[...].astype(F32) * score).astype(BF16)
        product(rows)

    score_row_ref[...] = jnp.broadcast_to(score, score_row_ref.shape)
    add_own_columns(map_ref, score_row_ref, lax.axis_index("cand"), lax.axis_index("mp"))
    weight = bias_ref[...] * score
    for bit, out_ref in enumerate(out_refs):
        size = out_ref.shape[0]
        block = aligned(lax.axis_index("cand") ^ bit, size)
        out_ref[:, pl.ds(0, columns)] = map_ref[block, :].astype(out_ref.dtype)
        total = jnp.zeros((size, LANES), F32)
        for start in range(0, width, LANES):
            cols = pl.ds(start, LANES)
            total = total + base_ref[block, cols].astype(F32) * weight[:, start : start + LANES]
        out_ref[:, pl.ds(columns, LANES)] = total.astype(out_ref.dtype)


def cross_scored(count, base_ref, bias_ref, *refs):
    part_refs, map_refs, (out_ref,) = refs[:count], refs[count : 2 * count], refs[2 * count :]
    size, width = part_refs[0].shape
    base = base_ref[aligned(lax.axis_index("cand"), size), :].astype(F32)
    once = (lax.axis_index("mp") == 0).astype(F32)

    def added(refs, cols):
        total = refs[0][:, cols].astype(F32)
        for ref in refs[1:]:
            total = total + ref[:, cols].astype(F32)
        return total

    score = added(map_refs, pl.ds(width, LANES)) * once
    for start in range(0, width, LANES):
        cols = pl.ds(start, LANES)
        cross = added(part_refs, cols) + base[:, start : start + LANES] * bias_ref[:, cols]
        rounded = cross.astype(BF16)
        out_ref[:, cols] = rounded
        score = score + rounded.astype(F32) * added(map_refs, cols)
    score = score[:, : LANES // 2] + score[:, LANES // 2 :]
    high = score.astype(BF16).astype(F32)
    both = jnp.concatenate([high, score - high], axis=1)
    out_ref[:, pl.ds(width, LANES)] = both.astype(BF16)


def assemble(*refs):
    *part_refs, rows_ref, logit_ref = refs
    width = rows_ref.shape[1]
    for bit, part_ref in enumerate(part_refs):
        block = lax.axis_index("cand") ^ bit
        rows_ref[aligned(block, part_ref.shape[0]), :] = part_ref[:, pl.ds(0, width)]
        lanes = part_ref[:, pl.ds(width, LANES)].astype(F32)
        logit_ref[pl.ds(block, 1), :] = jnp.sum(lanes.T, axis=0, keepdims=True)


def split_low(axis_bit, terms_ref, keep_ref, send_ref, size):
    for pair in range(keep_ref.shape[0] // size):
        rows = pl.ds(pair * size, size)
        keep_ref[rows, :] = terms_ref[aligned(2 * pair + axis_bit, size), :]
        send_ref[rows, :] = terms_ref[aligned(2 * pair + 1 - axis_bit, size), :].astype(BF16)


def layer_three(row_block, base_ref, weight_ref, rows_ref, keep_ref, send_ref, terms_ref):
    multiply(rows_ref, weight_ref, terms_ref, base_ref)
    model = lax.axis_index("mp")
    add_own_columns(terms_ref, rows_ref, model, lax.axis_index("cand"))
    split_low(model % 2, terms_ref, keep_ref, send_ref, row_block)


def halve(row_block, bit, keep_ref, other_ref, kept_ref, send_ref, terms_ref):
    terms_ref[...] = keep_ref[...] + other_ref[...].astype(F32)
    split_low((lax.axis_index("mp") // bit) % 2, terms_ref, kept_ref, send_ref, row_block)


def finish(keep_ref, other_ref, base_ref, bias_ref, total_ref, part_ref, out_ref, logit_ref, sum_ref):
    model = lax.axis_index("mp")
    base = base_ref[aligned(model, out_ref.shape[0]), :].astype(F32)
    cross = keep_ref[...] + other_ref[...].astype(F32) + base * bias_ref[...]
    out_ref[...] = cross.astype(BF16)
    sum_ref[...] = total_ref[...] + part_ref[...]
    logit_ref[...] = sum_ref[pl.ds(model, 1), :]


def finish_scored(keep_ref, other_ref, base_ref, bias_ref, score_ref, out_ref, logit_ref):
    base = base_ref[aligned(lax.axis_index("mp"), out_ref.shape[0]), :].astype(F32)
    cross = keep_ref[...] + other_ref[...].astype(F32) + base * bias_ref[...]
    out_ref[...] = cross.astype(BF16)
    logit_ref[...] = jnp.sum(cross * score_ref[...].astype(F32), axis=1, keepdims=True)


def body(
    user_feats,
    user_slot,
    cand_pool,
    cand_ids,
    first_weight,
    first_bias,
    second_weight,
    second_bias,
    third_weight,
    third_bias,
    score_weight,
):
    cand_count = lax.axis_size("cand")
    model_count = lax.axis_size("mp")
    local, half_width = user_feats.shape
    full_width = 2 * half_width
    user_count, per_user = cand_ids.shape
    row_total = user_count * per_user
    col_block = full_width // cand_count
    feat_block = full_width // model_count
    local_rows = row_total // cand_count
    row_block = row_total // model_count
    half_rows = row_total // 2
    flops = 2 * row_total * col_block * feat_block
    direct = cand_count == DIRECT and cand_count == model_count
    score, bias = score_weight.reshape(1, -1), third_bias.reshape(1, -1)

    if local > 1:
        user_feats = jnp.take(user_feats, user_slot % local, axis=0)
    elif user_count > 1:
        user_feats = jnp.broadcast_to(user_feats, (user_count, half_width))
    (staged,) = call(stage, [((8, 128), F32)], [], flops=STAGE_FLOPS)
    users = user_feats
    pool_model, pool_cand = call(
        functools.partial(choose_pool, half_width),
        [
            ((row_total, feat_block), BF16),
            ((row_total, col_block), BF16),
        ],
        [cand_ids, cand_pool, staged],
        limit=8 * MIB,
    )
    (want,) = call(
        functools.partial(owner_steps, local),
        [((user_count, 128), jnp.int32)],
        [user_slot],
        smem=(0,),
    )
    *bits, last_bit = bits_of(cand_count)
    if direct:
        users_other = swap(users, "cand", 1)
        (users,) = call(pair_rows, [((2 * user_count, half_width), BF16)], [users, users_other])
        bits = []
    for bit in bits:
        (users,) = call(
            functools.partial(choose_user, bit),
            [((user_count, half_width), BF16)],
            [want, users, swap(users, "cand", bit)],
        )
    users_other = swap(users, "cand", last_bit)

    half_outs = [((half_rows, col_block), F32), ((half_rows, col_block), BF16)]
    keep, send = call(
        functools.partial(pool_terms, half_width),
        half_outs,
        [pool_model, first_weight],
        scratch=[pltpu.VMEM((row_total, col_block), F32)],
        flops=flops,
        limit=12 * MIB,
    )
    for bit in bits_of(model_count):
        keep, send = call(add_up, half_outs, [keep, swap(send, "mp", bit)])
    pool_other = swap(send, "mp", 1)

    base_model, base_cand, user_sum = call(
        functools.partial(user_terms, half_width, last_bit),
        [
            ((row_total, feat_block), BF16),
            ((row_total, col_block), BF16),
            ((user_count, col_block), F32),
        ],
        [want, first_weight, pool_model, pool_cand, users, users_other],
        flops=flops,
        limit=12 * MIB,
    )
    *bits, last_bit = bits_of(model_count)
    for bit in bits:
        other = swap(user_sum, "mp", bit)
        (user_sum,) = call(add_to, [((user_count, col_block), F32)], [user_sum, other])
    user_other = swap(user_sum, "mp", last_bit)

    if direct:
        outs = [
            ((local_rows, feat_block + LANES), BF16 if bit else F32) for bit in range(cand_count)
        ]
        maps = call(
            functools.partial(score_map, half_width, user_count),
            outs,
            [base_cand, score, bias, third_weight],
            scratch=[
                pltpu.VMEM((row_total, col_block), BF16),
                pltpu.VMEM((row_total, feat_block), F32),
                pltpu.VMEM((row_total, col_block), F32),
            ],
            flops=flops,
            limit=12 * MIB,
        )
        maps = [maps[0]] + [swap(maps[bit], "cand", bit) for bit in range(1, cand_count)]
        outs = [((local_rows, feat_block), BF16 if bit else F32) for bit in range(cand_count)]
    else:
        outs = [((row_total, feat_block), BF16)]
    parts = call(
        layer_two,
        outs,
        [
            keep, pool_other, user_sum, user_other, first_bias.reshape(1, -1), base_cand,
            base_model, second_weight,
        ],
        scratch=[
            pltpu.VMEM((row_total, col_block), BF16),
            pltpu.VMEM((row_total, feat_block), F32),
            pltpu.VMEM((user_count, col_block), F32),
        ],
        flops=flops,
        limit=12 * MIB,
    )
    if direct:
        parts = [parts[0]] + [swap(parts[bit], "cand", bit) for bit in range(1, cand_count)]
    else:
        parts = [lax.psum_scatter(parts[0], "cand", scatter_dimension=0, tiled=True)]
    bias_two = second_bias.reshape(1, -1)
    if direct:
        (block,) = call(
            functools.partial(cross_scored, cand_count),
            [((local_rows, feat_block + LANES), BF16)],
            [base_model, bias_two, *parts, *maps],
        )
        parts = [block] + [swap(block, "cand", bit) for bit in range(1, cand_count)]
        logit_out = [((cand_count, local_rows), F32)]
        cross_two, logits = call(assemble, [((row_total, feat_block), BF16)] + logit_out, parts)
    else:
        (block,) = call(
            cross_rows, [((local_rows, feat_block), BF16)], [base_model, bias_two, *parts]
        )
        cross_two = lax.all_gather(block, "cand", axis=0, tiled=True)
    rows = row_total // 2
    keep, send = call(
        functools.partial(layer_three, row_block),
        [((rows, col_block), F32), ((rows, col_block), BF16)],
        [base_cand, third_weight, cross_two],
        scratch=[pltpu.VMEM((row_total, col_block), F32)],
        flops=flops,
        limit=12 * MIB,
    )
    other = swap(send, "mp", 1)
    for bit in bits_of(model_count)[1:]:
        scratch = [pltpu.VMEM((rows, col_block), F32)]
        rows //= 2
        keep, send = call(
            functools.partial(halve, row_block, bit),
            [((rows, col_block), F32), ((rows, col_block), BF16)],
            [keep, other],
            scratch=scratch,
        )
        other = swap(send, "mp", bit)

    rows = [keep, other, base_cand, bias]
    crossed_out = ((row_block, col_block), BF16)
    if direct:
        for bit in bits:
            (logits,) = call(add_to, logit_out, [logits, swap(logits, "mp", bit)])
        crossed, logits = call(
            finish,
            [crossed_out, ((1, row_block), F32)],
            [*rows, logits, swap(logits, "mp", last_bit)],
            scratch=[pltpu.VMEM((cand_count, local_rows), F32)],
        )
    else:
        crossed, logits = call(finish_scored, [crossed_out, ((row_block, 1), F32)], [*rows, score])
        logits = lax.psum(logits, "cand")
    return (crossed, logits.reshape(-1))


def solution(mesh):
    in_specs = (
        P(("groups", "cand"), None),
        P("groups"),
        P("groups", None),
        P("groups", None),
        P("mp", "cand"),
        P("cand"),
        P("cand", "mp"),
        P("mp"),
        P("mp", "cand"),
        P("cand"),
        P("cand"),
    )
    out_specs = (P(("groups", "mp"), "cand"), P(("groups", "mp")))

    return jax.shard_map(body, mesh=mesh, in_specs=in_specs, out_specs=out_specs, check_vma=False)
```

```python
import functools

import jax
import jax.numpy as jnp
from jax import lax
from jax.experimental import pallas as pl
from jax.experimental.pallas import tpu as pltpu
from jax.sharding import PartitionSpec as P


F32 = jnp.float32
BF16 = jnp.bfloat16
LANES = 128
DIRECT = 4
MIB = 1024 * 1024
STAGE_FLOPS = 1 << 34


def bits_of(count):
    bits, bit = [], 1
    while bit < count:
        bits.append(bit)
        bit *= 2
    assert bit == count
    return bits


def swap(value, axis, bit):
    count = lax.axis_size(axis)
    return lax.ppermute(value, axis, [(i, i ^ bit) for i in range(count)])


def call(kernel, outs, args, scratch=(), hbm=(), smem=(), flops=0, limit=6 * MIB):
    moved = sum(a.size * a.dtype.itemsize for a in args if a.size < 2 * MIB)
    moved += sum(functools.reduce(lambda a, b: a * b, s) * jnp.dtype(d).itemsize for s, d in outs)
    return pl.pallas_call(
        kernel,
        out_shape=[jax.ShapeDtypeStruct(s, d) for s, d in outs],
        in_specs=[
            pl.BlockSpec(
                memory_space=pltpu.HBM if i in hbm else pltpu.SMEM if i in smem else pltpu.VMEM
            )
            for i in range(len(args))
        ],
        out_specs=[pl.BlockSpec(memory_space=pltpu.VMEM)] * len(outs),
        scratch_shapes=list(scratch),
        compiler_params=pltpu.CompilerParams(vmem_limit_bytes=limit),
        cost_estimate=pl.CostEstimate(flops=flops, bytes_accessed=moved, transcendentals=0),
    )(*[pltpu.with_memory_space_constraint(a, pltpu.HBM) if i in hbm else a for i, a in enumerate(args)])


def aligned(index, size):
    return pl.ds(pl.multiple_of(index * size, size), size)


def add_to(*refs):
    *part_refs, out_ref = refs
    total = part_refs[0][...]
    for part_ref in part_refs[1:]:
        total = total + part_ref[...]
    out_ref[...] = total


def stage(out_ref):
    out_ref[...] = jnp.zeros_like(out_ref)


def choose_user(local, bit, slot_ref, own_ref, other_ref, out_ref):
    want = (slot_ref[...] // local) ^ lax.axis_index("cand")
    other, own = other_ref[...].astype(F32), own_ref[...].astype(F32)
    out_ref[...] = jnp.where((jnp.broadcast_to(want, own.shape) & bit) != 0, other, own).astype(BF16)


def owner_steps(local, slot_ref, out_ref):
    row = lax.broadcasted_iota(jnp.int32, out_ref.shape, 0)
    want = jnp.zeros(out_ref.shape, jnp.int32)
    for user in range(out_ref.shape[0]):
        owner = lax.div(slot_ref[user], local) ^ lax.axis_index("cand")
        want = jnp.where(row == user, owner, want)
    out_ref[...] = want


def choose_pool(
    half, ids_ref, pool_ref, _, model_ref, cand_ref
):
    users, rows = ids_ref.shape
    numbers = lax.broadcasted_iota(jnp.int32, (pool_ref.shape[0], rows), 0)
    for axis, out_ref in (("mp", model_ref), ("cand", cand_ref)):
        width = out_ref.shape[1]
        cols = aligned(lax.axis_index(axis) % (half // width), width)
        for user in range(users):
            chosen = (numbers == ids_ref[pl.ds(user, 1), :]).astype(BF16)
            out_ref[pl.ds(user * rows, rows), :] = lax.dot_general(
                chosen, pool_ref[:, cols], (((0,), (0,)), ((), ())), preferred_element_type=F32
            ).astype(BF16)


def tiles(width, step=512):
    step = min(step, width)
    return [pl.ds(i, step) for i in range(0, width, step)]


def multiply(rows_ref, weight_ref, out_ref, scale_ref=None):
    for cols in tiles(out_ref.shape[1]):
        value = jnp.dot(rows_ref[...], weight_ref[:, cols], preferred_element_type=F32)
        out_ref[:, cols] = value if scale_ref is None else scale_ref[:, cols].astype(F32) * value


def pool_terms(half, rows_ref, weight_ref, keep_ref, send_ref, terms_ref):
    inside = lax.axis_index("mp") < half // rows_ref.shape[1]

    @pl.when(inside)
    def _():
        keep_ref[...] = jnp.zeros_like(keep_ref)
        send_ref[...] = jnp.zeros_like(send_ref)

    @pl.when(jnp.logical_not(inside))
    def _():
        multiply(rows_ref, weight_ref, terms_ref)
        low = lax.axis_index("mp") % 2
        size = keep_ref.shape[0]
        keep_ref[...] = terms_ref[aligned(low, size), :]
        send_ref[...] = terms_ref[aligned(1 - low, size), :].astype(BF16)


def user_terms(
    half, want_ref, weight_ref, pool_model_ref, pool_cand_ref, *refs
):
    *part_refs, model_ref, cand_ref, terms_ref = refs
    users = part_refs[0].shape[0]
    terms_ref[...] = jnp.zeros_like(terms_ref)
    for axis, pool_ref, out_ref in (
        ("mp", pool_model_ref, model_ref),
        ("cand", pool_cand_ref, cand_ref),
    ):
        rows, width = out_ref.shape
        block = lax.axis_index(axis)
        inside = block < half // width

        @pl.when(inside)
        def _():
            cols = aligned(block % (half // width), width)
            parts = [part_ref[:, cols] for part_ref in part_refs]
            chosen = parts[0].astype(F32)
            want = jnp.broadcast_to(want_ref[:, :1], chosen.shape)
            for bit in range(1, len(parts)):
                chosen = jnp.where(want == bit, parts[bit].astype(F32), chosen)
            for user in range(users):
                out_ref[pl.ds(user * (rows // users), rows // users), :] = jnp.broadcast_to(
                    chosen[user : user + 1], (rows // users, width)
                ).astype(BF16)
            if axis == "mp":
                padded = chosen
                if users < 8:
                    padded = jnp.concatenate([chosen, jnp.zeros((8 - users, width), F32)], axis=0)
                padded = padded.astype(BF16)
                for tile in tiles(terms_ref.shape[1]):
                    value = jnp.dot(padded, weight_ref[:, tile], preferred_element_type=F32)
                    terms_ref[:, tile] = value[:users]

        @pl.when(jnp.logical_not(inside))
        def _():
            out_ref[...] = pool_ref[...]


def add_up(keep_ref, other_ref, sum_ref, send_ref):
    total = keep_ref[...] + other_ref[...].astype(F32)
    sum_ref[...] = total
    send_ref[...] = total.astype(BF16)


def merge(keep_ref, other_ref, user_ref, user_other_ref, sum_ref, send_ref, users_ref):
    low = lax.axis_index("mp") % 2
    size, users = keep_ref.shape[0], user_ref.shape[0]
    assert users == 1 or users % 2 == 0
    users_ref[...] = user_ref[...] + user_other_ref[...]
    each = max(users // 2, 1)
    for piece in range(each):
        user = low * each + piece if users > 1 else 0
        part = pl.ds(piece * (size // each), size // each)
        total = keep_ref[part, :] + other_ref[part, :].astype(F32) + users_ref[pl.ds(user, 1), :]
        sum_ref[part, :] = total
        send_ref[part, :] = total.astype(BF16)


def add_own_columns(terms_ref, rows_ref, have, want):
    width, wanted = rows_ref.shape[1], terms_ref.shape[1]
    small = min(width, wanted)
    ratio = max(width, wanted) // small
    assert max(width, wanted) == ratio * small
    if width >= wanted:
        inside, here, there = want // ratio == have, aligned(want % ratio, small), slice(None)
    else:
        inside, here, there = have // ratio == want, slice(None), aligned(have % ratio, small)

    @pl.when(inside)
    def _():
        terms_ref[:, there] += rows_ref[:, here].astype(F32)


def layer_two(mine_ref, other_ref, bias_ref, cand_ref, base_ref, weight_ref, *refs):
    *out_refs, rows_ref, terms_ref = refs
    low = lax.axis_index("mp") % 2
    size = mine_ref.shape[0]
    for index, sum_ref in ((low, mine_ref), (1 - low, other_ref)):
        here = aligned(index, size)
        base = cand_ref[here, :].astype(F32)
        total = sum_ref[...].astype(F32) + bias_ref[...]
        rows_ref[here, :] = (base * total + base).astype(BF16)
    multiply(rows_ref, weight_ref, terms_ref, base_ref)
    cand = lax.axis_index("cand")
    add_own_columns(terms_ref, rows_ref, cand, lax.axis_index("mp"))
    if len(out_refs) == 1:
        out_refs[0][...] = terms_ref[...].astype(BF16)
        return
    for bit, out_ref in enumerate(out_refs):
        out_ref[...] = terms_ref[aligned(cand ^ bit, out_ref.shape[0]), :].astype(out_ref.dtype)


def cross_rows(base_ref, bias_ref, *refs):
    *part_refs, out_ref = refs
    total = part_refs[0][...].astype(F32)
    for part_ref in part_refs[1:]:
        total = total + part_ref[...].astype(F32)
    base = base_ref[aligned(lax.axis_index("cand"), out_ref.shape[0]), :].astype(F32)
    out_ref[...] = (total + base * bias_ref[...]).astype(BF16)


def score_map(half, users, base_ref, score_ref, bias_ref, weight_ref, *refs):
    *out_refs, rows_ref, map_ref, score_row_ref = refs
    rows, width = base_ref.shape
    columns = map_ref.shape[1]
    each = rows // users
    inside = lax.axis_index("cand") < half // width
    score = score_ref[...].astype(F32)

    def product(count):
        for part in tiles(columns):
            map_ref[pl.ds(0, count), part] = lax.dot_general(
                rows_ref[pl.ds(0, count), :],
                weight_ref[part, :],
                (((1,), (1,)), ((), ())),
                preferred_element_type=F32,
            )

    @pl.when(inside)
    def _():
        small = max(users, 16)
        score_row_ref[pl.ds(0, small), :] = jnp.zeros((small, width), F32)
        for user in range(users):
            base = base_ref[pl.ds(user * each, each), :].astype(F32)[:1]
            score_row_ref[pl.ds(user, 1), :] = base * score
        rows_ref[pl.ds(0, small), :] = score_row_ref[pl.ds(0, small), :].astype(BF16)
        product(small)
        for user in reversed(range(users)):
            row = map_ref[pl.ds(user, 1), :]
            map_ref[pl.ds(user * each, each), :] = jnp.broadcast_to(row, (each, columns))

    @pl.when(jnp.logical_not(inside))
    def _():
        rows_ref[...] = (base_ref[...].astype(F32) * score).astype(BF16)
        product(rows)

    score_row_ref[...] = jnp.broadcast_to(score, score_row_ref.shape)
    add_own_columns(map_ref, score_row_ref, lax.axis_index("cand"), lax.axis_index("mp"))
    weight = bias_ref[...] * score
    for bit, out_ref in enumerate(out_refs):
        size = out_ref.shape[0]
        block = aligned(lax.axis_index("cand") ^ bit, size)
        out_ref[:, pl.ds(0, columns)] = map_ref[block, :].astype(out_ref.dtype)
        total = jnp.zeros((size, LANES), F32)
        for start in range(0, width, LANES):
            cols = pl.ds(start, LANES)
            total = total + base_ref[block, cols].astype(F32) * weight[:, start : start + LANES]
        out_ref[:, pl.ds(columns, LANES)] = total.astype(out_ref.dtype)


def cross_scored(count, base_ref, bias_ref, *refs):
    part_refs, map_refs, (out_ref,) = refs[:count], refs[count : 2 * count], refs[2 * count :]
    size, width = part_refs[0].shape
    base = base_ref[aligned(lax.axis_index("cand"), size), :].astype(F32)
    once = (lax.axis_index("mp") == 0).astype(F32)

    def added(refs, cols):
        total = refs[0][:, cols].astype(F32)
        for ref in refs[1:]:
            total = total + ref[:, cols].astype(F32)
        return total

    score = added(map_refs, pl.ds(width, LANES)) * once
    for start in range(0, width, LANES):
        cols = pl.ds(start, LANES)
        cross = added(part_refs, cols) + base[:, start : start + LANES] * bias_ref[:, cols]
        rounded = cross.astype(BF16)
        out_ref[:, cols] = rounded
        score = score + rounded.astype(F32) * added(map_refs, cols)
    score = score[:, : LANES // 2] + score[:, LANES // 2 :]
    high = score.astype(BF16).astype(F32)
    both = jnp.concatenate([high, score - high], axis=1)
    out_ref[:, pl.ds(width, LANES)] = both.astype(BF16)


def assemble(*refs):
    *part_refs, rows_ref, logit_ref = refs
    width = rows_ref.shape[1]
    for bit, part_ref in enumerate(part_refs):
        block = lax.axis_index("cand") ^ bit
        rows_ref[aligned(block, part_ref.shape[0]), :] = part_ref[:, pl.ds(0, width)]
        lanes = part_ref[:, pl.ds(width, LANES)].astype(F32)
        logit_ref[pl.ds(block, 1), :] = jnp.sum(lanes.T, axis=0, keepdims=True)


def split_low(axis_bit, terms_ref, keep_ref, send_ref, size):
    for pair in range(keep_ref.shape[0] // size):
        rows = pl.ds(pair * size, size)
        keep_ref[rows, :] = terms_ref[aligned(2 * pair + axis_bit, size), :]
        send_ref[rows, :] = terms_ref[aligned(2 * pair + 1 - axis_bit, size), :].astype(BF16)


def layer_three(row_block, base_ref, weight_ref, rows_ref, keep_ref, send_ref, terms_ref):
    multiply(rows_ref, weight_ref, terms_ref, base_ref)
    model = lax.axis_index("mp")
    add_own_columns(terms_ref, rows_ref, model, lax.axis_index("cand"))
    split_low(model % 2, terms_ref, keep_ref, send_ref, row_block)


def halve(row_block, bit, keep_ref, other_ref, kept_ref, send_ref, terms_ref):
    terms_ref[...] = keep_ref[...] + other_ref[...].astype(F32)
    split_low((lax.axis_index("mp") // bit) % 2, terms_ref, kept_ref, send_ref, row_block)


def finish(keep_ref, other_ref, base_ref, bias_ref, total_ref, part_ref, out_ref, logit_ref, sum_ref):
    model = lax.axis_index("mp")
    base = base_ref[aligned(model, out_ref.shape[0]), :].astype(F32)
    cross = keep_ref[...] + other_ref[...].astype(F32) + base * bias_ref[...]
    out_ref[...] = cross.astype(BF16)
    sum_ref[...] = total_ref[...] + part_ref[...]
    logit_ref[...] = sum_ref[pl.ds(model, 1), :]


def finish_scored(keep_ref, other_ref, base_ref, bias_ref, score_ref, out_ref, logit_ref):
    base = base_ref[aligned(lax.axis_index("mp"), out_ref.shape[0]), :].astype(F32)
    cross = keep_ref[...] + other_ref[...].astype(F32) + base * bias_ref[...]
    out_ref[...] = cross.astype(BF16)
    logit_ref[...] = jnp.sum(cross * score_ref[...].astype(F32), axis=1, keepdims=True)


def body(
    user_feats,
    user_slot,
    cand_pool,
    cand_ids,
    first_weight,
    first_bias,
    second_weight,
    second_bias,
    third_weight,
    third_bias,
    score_weight,
):
    cand_count = lax.axis_size("cand")
    model_count = lax.axis_size("mp")
    local, half_width = user_feats.shape
    full_width = 2 * half_width
    user_count, per_user = cand_ids.shape
    row_total = user_count * per_user
    col_block = full_width // cand_count
    feat_block = full_width // model_count
    local_rows = row_total // cand_count
    row_block = row_total // model_count
    half_rows = row_total // 2
    flops = 2 * row_total * col_block * feat_block
    direct = cand_count <= DIRECT and cand_count == model_count
    score, bias = score_weight.reshape(1, -1), third_bias.reshape(1, -1)

    if local > 1:
        user_feats = jnp.take(user_feats, user_slot % local, axis=0)
    elif user_count > 1:
        user_feats = jnp.broadcast_to(user_feats, (user_count, half_width))
    (staged,) = call(stage, [((8, 128), F32)], [], flops=STAGE_FLOPS)
    users = user_feats
    pool_model, pool_cand = call(
        functools.partial(choose_pool, half_width),
        [
            ((row_total, feat_block), BF16),
            ((row_total, col_block), BF16),
        ],
        [cand_ids, cand_pool, staged],
        limit=8 * MIB,
    )
    (want,) = call(
        functools.partial(owner_steps, local),
        [((user_count, 128), jnp.int32)],
        [user_slot],
        smem=(0,),
    )
    if direct:
        users = [users] + [swap(users, "cand", bit) for bit in range(1, cand_count)]
    else:
        slots = user_slot.reshape(-1, 1)
        for bit in bits_of(cand_count):
            (users,) = call(
                functools.partial(choose_user, local, bit),
                [((user_count, half_width), BF16)],
                [slots, users, swap(users, "cand", bit)],
            )
        users = [users]

    half_outs = [((half_rows, col_block), F32), ((half_rows, col_block), BF16)]
    keep, send = call(
        functools.partial(pool_terms, half_width),
        half_outs,
        [pool_model, first_weight],
        scratch=[pltpu.VMEM((row_total, col_block), F32)],
        flops=flops,
        limit=12 * MIB,
    )
    base_model, base_cand, user_sum = call(
        functools.partial(user_terms, half_width),
        [
            ((row_total, feat_block), BF16),
            ((row_total, col_block), BF16),
            ((user_count, col_block), F32),
        ],
        [want, first_weight, pool_model, pool_cand, *users],
        flops=flops,
        limit=12 * MIB,
    )
    *bits, last_bit = bits_of(model_count)
    assert bits
    for bit in bits:
        other = swap(send, "mp", bit)
        user_other = swap(user_sum, "mp", bit)
        if bit == bits[-1]:
            keep, send = call(
                merge,
                half_outs,
                [keep, other, user_sum, user_other],
                scratch=[pltpu.VMEM((user_count, col_block), F32)],
            )
        else:
            keep, send = call(add_up, half_outs, [keep, other])
            (user_sum,) = call(
                add_to, [((user_count, col_block), F32)], [user_sum, user_other]
            )
    keep, send = call(add_up, half_outs, [keep, swap(send, "mp", last_bit)])
    pool_other = swap(send, "mp", 1)

    if direct:
        outs = [
            ((local_rows, feat_block + LANES), BF16 if bit else F32) for bit in range(cand_count)
        ]
        maps = call(
            functools.partial(score_map, half_width, user_count),
            outs,
            [base_cand, score, bias, third_weight],
            scratch=[
                pltpu.VMEM((row_total, col_block), BF16),
                pltpu.VMEM((row_total, feat_block), F32),
                pltpu.VMEM((row_total, col_block), F32),
            ],
            flops=flops,
            limit=12 * MIB,
        )
        maps = [maps[0]] + [swap(maps[bit], "cand", bit) for bit in range(1, cand_count)]
        outs = [((local_rows, feat_block), BF16 if bit else F32) for bit in range(cand_count)]
    else:
        outs = [((row_total, feat_block), BF16)]
    parts = call(
        layer_two,
        outs,
        [
            keep, pool_other, first_bias.reshape(1, -1), base_cand, base_model, second_weight,
        ],
        scratch=[
            pltpu.VMEM((row_total, col_block), BF16),
            pltpu.VMEM((row_total, feat_block), F32),
        ],
        flops=flops,
        limit=12 * MIB,
    )
    if direct:
        parts = [parts[0]] + [swap(parts[bit], "cand", bit) for bit in range(1, cand_count)]
    else:
        parts = [lax.psum_scatter(parts[0], "cand", scatter_dimension=0, tiled=True)]
    bias_two = second_bias.reshape(1, -1)
    if direct:
        (block,) = call(
            functools.partial(cross_scored, cand_count),
            [((local_rows, feat_block + LANES), BF16)],
            [base_model, bias_two, *parts, *maps],
        )
        parts = [block] + [swap(block, "cand", bit) for bit in range(1, cand_count)]
        logit_out = [((cand_count, local_rows), F32)]
        cross_two, logits = call(assemble, [((row_total, feat_block), BF16)] + logit_out, parts)
    else:
        (block,) = call(
            cross_rows, [((local_rows, feat_block), BF16)], [base_model, bias_two, *parts]
        )
        cross_two = lax.all_gather(block, "cand", axis=0, tiled=True)
    rows = row_total // 2
    keep, send = call(
        functools.partial(layer_three, row_block),
        [((rows, col_block), F32), ((rows, col_block), BF16)],
        [base_cand, third_weight, cross_two],
        scratch=[pltpu.VMEM((row_total, col_block), F32)],
        flops=flops,
        limit=12 * MIB,
    )
    other = swap(send, "mp", 1)
    for bit in bits_of(model_count)[1:]:
        scratch = [pltpu.VMEM((rows, col_block), F32)]
        rows //= 2
        keep, send = call(
            functools.partial(halve, row_block, bit),
            [((rows, col_block), F32), ((rows, col_block), BF16)],
            [keep, other],
            scratch=scratch,
        )
        other = swap(send, "mp", bit)

    rows = [keep, other, base_cand, bias]
    crossed_out = ((row_block, col_block), BF16)
    if direct:
        for bit in bits:
            (logits,) = call(add_to, logit_out, [logits, swap(logits, "mp", bit)])
        crossed, logits = call(
            finish,
            [crossed_out, ((1, row_block), F32)],
            [*rows, logits, swap(logits, "mp", last_bit)],
            scratch=[pltpu.VMEM((cand_count, local_rows), F32)],
        )
    else:
        crossed, logits = call(finish_scored, [crossed_out, ((row_block, 1), F32)], [*rows, score])
        logits = lax.psum(logits, "cand")
    return (crossed, logits.reshape(-1))


def solution(mesh):
    in_specs = (
        P(("groups", "cand"), None),
        P("groups"),
        P("groups", None),
        P("groups", None),
        P("mp", "cand"),
        P("cand"),
        P("cand", "mp"),
        P("mp"),
        P("mp", "cand"),
        P("cand"),
        P("cand"),
    )
    out_specs = (P(("groups", "mp"), "cand"), P(("groups", "mp")))

    return jax.shard_map(body, mesh=mesh, in_specs=in_specs, out_specs=out_specs, check_vma=False)
```

```python
import functools

import jax
import jax.numpy as jnp
from jax import lax
from jax.experimental import pallas as pl
from jax.experimental.pallas import tpu as pltpu
from jax.sharding import PartitionSpec as P


F32 = jnp.float32
BF16 = jnp.bfloat16
LANES = 128
DIRECT = 4
MIB = 1024 * 1024
STAGE_FLOPS = 1 << 34


def bits_of(count):
    bits, bit = [], 1
    while bit < count:
        bits.append(bit)
        bit *= 2
    assert bit == count
    return bits


def swap(value, axis, bit):
    count = lax.axis_size(axis)
    return lax.ppermute(value, axis, [(i, i ^ bit) for i in range(count)])


def call(kernel, outs, args, scratch=(), hbm=(), smem=(), flops=0, limit=6 * MIB):
    moved = sum(a.size * a.dtype.itemsize for a in args if a.size < 2 * MIB)
    moved += sum(functools.reduce(lambda a, b: a * b, s) * jnp.dtype(d).itemsize for s, d in outs)
    return pl.pallas_call(
        kernel,
        out_shape=[jax.ShapeDtypeStruct(s, d) for s, d in outs],
        in_specs=[
            pl.BlockSpec(
                memory_space=pltpu.HBM if i in hbm else pltpu.SMEM if i in smem else pltpu.VMEM
            )
            for i in range(len(args))
        ],
        out_specs=[pl.BlockSpec(memory_space=pltpu.VMEM)] * len(outs),
        scratch_shapes=list(scratch),
        compiler_params=pltpu.CompilerParams(vmem_limit_bytes=limit),
        cost_estimate=pl.CostEstimate(flops=flops, bytes_accessed=moved, transcendentals=0),
    )(*[pltpu.with_memory_space_constraint(a, pltpu.HBM) if i in hbm else a for i, a in enumerate(args)])


def aligned(index, size):
    return pl.ds(pl.multiple_of(index * size, size), size)


def add_to(*refs):
    *part_refs, out_ref = refs
    total = part_refs[0][...]
    for part_ref in part_refs[1:]:
        total = total + part_ref[...]
    out_ref[...] = total


def stage(out_ref):
    out_ref[...] = jnp.zeros_like(out_ref)


def choose_user(local, bit, slot_ref, own_ref, other_ref, out_ref):
    want = (slot_ref[...] // local) ^ lax.axis_index("cand")
    other, own = other_ref[...].astype(F32), own_ref[...].astype(F32)
    out_ref[...] = jnp.where((jnp.broadcast_to(want, own.shape) & bit) != 0, other, own).astype(BF16)


def owner_steps(local, slot_ref, out_ref):
    row = lax.broadcasted_iota(jnp.int32, out_ref.shape, 0)
    want = jnp.zeros(out_ref.shape, jnp.int32)
    for user in range(out_ref.shape[0]):
        owner = lax.div(slot_ref[user], local) ^ lax.axis_index("cand")
        want = jnp.where(row == user, owner, want)
    out_ref[...] = want


def choose_pool(
    half, ids_ref, pool_ref, _, model_ref, cand_ref
):
    users, rows = ids_ref.shape
    numbers = lax.broadcasted_iota(jnp.int32, (pool_ref.shape[0], rows), 0)
    for axis, out_ref in (("mp", model_ref), ("cand", cand_ref)):
        width = out_ref.shape[1]
        cols = aligned(lax.axis_index(axis) % (half // width), width)
        for user in range(users):
            chosen = (numbers == ids_ref[pl.ds(user, 1), :]).astype(BF16)
            out_ref[pl.ds(user * rows, rows), :] = lax.dot_general(
                chosen, pool_ref[:, cols], (((0,), (0,)), ((), ())), preferred_element_type=F32
            ).astype(BF16)


def tiles(width, step=512):
    step = min(step, width)
    return [pl.ds(i, step) for i in range(0, width, step)]


def multiply(rows_ref, weight_ref, out_ref, scale_ref=None):
    for cols in tiles(out_ref.shape[1]):
        value = jnp.dot(rows_ref[...], weight_ref[:, cols], preferred_element_type=F32)
        out_ref[:, cols] = value if scale_ref is None else scale_ref[:, cols].astype(F32) * value


def pool_terms(half, rows_ref, weight_ref, keep_ref, send_ref, terms_ref):
    inside = lax.axis_index("mp") < half // rows_ref.shape[1]

    @pl.when(inside)
    def _():
        keep_ref[...] = jnp.zeros_like(keep_ref)
        send_ref[...] = jnp.zeros_like(send_ref)

    @pl.when(jnp.logical_not(inside))
    def _():
        multiply(rows_ref, weight_ref, terms_ref)
        low = lax.axis_index("mp") % 2
        size = keep_ref.shape[0]
        keep_ref[...] = terms_ref[aligned(low, size), :]
        send_ref[...] = terms_ref[aligned(1 - low, size), :].astype(BF16)


def user_terms(
    half, want_ref, weight_ref, pool_model_ref, pool_cand_ref, *refs
):
    *part_refs, model_ref, cand_ref, terms_ref = refs
    users = part_refs[0].shape[0]
    terms_ref[...] = jnp.zeros_like(terms_ref)
    for axis, pool_ref, out_ref in (
        ("mp", pool_model_ref, model_ref),
        ("cand", pool_cand_ref, cand_ref),
    ):
        rows, width = out_ref.shape
        block = lax.axis_index(axis)
        inside = block < half // width

        @pl.when(inside)
        def _():
            cols = aligned(block % (half // width), width)
            parts = [part_ref[:, cols] for part_ref in part_refs]
            chosen = parts[0].astype(F32)
            want = jnp.broadcast_to(want_ref[:, :1], chosen.shape)
            for bit in range(1, len(parts)):
                chosen = jnp.where(want == bit, parts[bit].astype(F32), chosen)
            for user in range(users):
                out_ref[pl.ds(user * (rows // users), rows // users), :] = jnp.broadcast_to(
                    chosen[user : user + 1], (rows // users, width)
                ).astype(BF16)
            if axis == "mp":
                padded = chosen
                if users < 8:
                    padded = jnp.concatenate([chosen, jnp.zeros((8 - users, width), F32)], axis=0)
                padded = padded.astype(BF16)
                for tile in tiles(terms_ref.shape[1]):
                    value = jnp.dot(padded, weight_ref[:, tile], preferred_element_type=F32)
                    terms_ref[:, tile] = value[:users]

        @pl.when(jnp.logical_not(inside))
        def _():
            out_ref[...] = pool_ref[...]


def add_up(keep_ref, other_ref, sum_ref, send_ref):
    total = keep_ref[...] + other_ref[...].astype(F32)
    sum_ref[...] = total
    send_ref[...] = total.astype(BF16)


def merge(keep_ref, part_ref, user_ref, sum_ref, send_ref):
    low = lax.axis_index("mp") % 2
    size, users = keep_ref.shape[0], user_ref.shape[0]
    assert users == 1 or users % 2 == 0
    each = max(users // 2, 1)
    for index, in_ref, out_ref in ((low, keep_ref, sum_ref), (1 - low, part_ref, send_ref)):
        for piece in range(each):
            user = index * each + piece if users > 1 else 0
            part = pl.ds(piece * (size // each), size // each)
            total = in_ref[part, :].astype(F32) + user_ref[pl.ds(user, 1), :]
            out_ref[part, :] = total.astype(out_ref.dtype)


def add_own_columns(terms_ref, rows_ref, have, want):
    width, wanted = rows_ref.shape[1], terms_ref.shape[1]
    small = min(width, wanted)
    ratio = max(width, wanted) // small
    assert max(width, wanted) == ratio * small
    if width >= wanted:
        inside, here, there = want // ratio == have, aligned(want % ratio, small), slice(None)
    else:
        inside, here, there = have // ratio == want, slice(None), aligned(have % ratio, small)

    @pl.when(inside)
    def _():
        terms_ref[:, there] += rows_ref[:, here].astype(F32)


def layer_two(mine_ref, other_ref, bias_ref, cand_ref, base_ref, weight_ref, *refs):
    *out_refs, rows_ref, terms_ref = refs
    low = lax.axis_index("mp") % 2
    size = mine_ref.shape[0]
    for index, sum_ref in ((low, mine_ref), (1 - low, other_ref)):
        here = aligned(index, size)
        base = cand_ref[here, :].astype(F32)
        total = sum_ref[...].astype(F32) + bias_ref[...]
        rows_ref[here, :] = (base * total + base).astype(BF16)
    multiply(rows_ref, weight_ref, terms_ref, base_ref)
    cand = lax.axis_index("cand")
    add_own_columns(terms_ref, rows_ref, cand, lax.axis_index("mp"))
    if len(out_refs) == 1:
        out_refs[0][...] = terms_ref[...].astype(BF16)
        return
    for bit, out_ref in enumerate(out_refs):
        out_ref[...] = terms_ref[aligned(cand ^ bit, out_ref.shape[0]), :].astype(out_ref.dtype)


def cross_rows(base_ref, bias_ref, *refs):
    *part_refs, out_ref = refs
    total = part_refs[0][...].astype(F32)
    for part_ref in part_refs[1:]:
        total = total + part_ref[...].astype(F32)
    base = base_ref[aligned(lax.axis_index("cand"), out_ref.shape[0]), :].astype(F32)
    out_ref[...] = (total + base * bias_ref[...]).astype(BF16)


def score_map(half, users, base_ref, score_ref, bias_ref, weight_ref, *refs):
    *out_refs, rows_ref, map_ref, score_row_ref = refs
    rows, width = base_ref.shape
    columns = map_ref.shape[1]
    each = rows // users
    inside = lax.axis_index("cand") < half // width
    score = score_ref[...].astype(F32)

    def product(count):
        for part in tiles(columns):
            map_ref[pl.ds(0, count), part] = lax.dot_general(
                rows_ref[pl.ds(0, count), :],
                weight_ref[part, :],
                (((1,), (1,)), ((), ())),
                preferred_element_type=F32,
            )

    @pl.when(inside)
    def _():
        small = max(users, 16)
        score_row_ref[pl.ds(0, small), :] = jnp.zeros((small, width), F32)
        for user in range(users):
            base = base_ref[pl.ds(user * each, each), :].astype(F32)[:1]
            score_row_ref[pl.ds(user, 1), :] = base * score
        rows_ref[pl.ds(0, small), :] = score_row_ref[pl.ds(0, small), :].astype(BF16)
        product(small)
        for user in reversed(range(users)):
            row = map_ref[pl.ds(user, 1), :]
            map_ref[pl.ds(user * each, each), :] = jnp.broadcast_to(row, (each, columns))

    @pl.when(jnp.logical_not(inside))
    def _():
        rows_ref[...] = (base_ref[...].astype(F32) * score).astype(BF16)
        product(rows)

    score_row_ref[...] = jnp.broadcast_to(score, score_row_ref.shape)
    add_own_columns(map_ref, score_row_ref, lax.axis_index("cand"), lax.axis_index("mp"))
    weight = bias_ref[...] * score
    for bit, out_ref in enumerate(out_refs):
        size = out_ref.shape[0]
        block = aligned(lax.axis_index("cand") ^ bit, size)
        out_ref[:, pl.ds(0, columns)] = map_ref[block, :].astype(out_ref.dtype)
        total = jnp.zeros((size, LANES), F32)
        for start in range(0, width, LANES):
            cols = pl.ds(start, LANES)
            total = total + base_ref[block, cols].astype(F32) * weight[:, start : start + LANES]
        out_ref[:, pl.ds(columns, LANES)] = total.astype(out_ref.dtype)


def cross_scored(count, base_ref, bias_ref, *refs):
    part_refs, map_refs, (out_ref,) = refs[:count], refs[count : 2 * count], refs[2 * count :]
    size, width = part_refs[0].shape
    base = base_ref[aligned(lax.axis_index("cand"), size), :].astype(F32)
    once = (lax.axis_index("mp") == 0).astype(F32)

    def added(refs, cols):
        total = refs[0][:, cols].astype(F32)
        for ref in refs[1:]:
            total = total + ref[:, cols].astype(F32)
        return total

    score = added(map_refs, pl.ds(width, LANES)) * once
    for start in range(0, width, LANES):
        cols = pl.ds(start, LANES)
        cross = added(part_refs, cols) + base[:, start : start + LANES] * bias_ref[:, cols]
        rounded = cross.astype(BF16)
        out_ref[:, cols] = rounded
        score = score + rounded.astype(F32) * added(map_refs, cols)
    score = score[:, : LANES // 2] + score[:, LANES // 2 :]
    high = score.astype(BF16).astype(F32)
    both = jnp.concatenate([high, score - high], axis=1)
    out_ref[:, pl.ds(width, LANES)] = both.astype(BF16)


def assemble(*refs):
    *part_refs, rows_ref, logit_ref = refs
    width = rows_ref.shape[1]
    for bit, part_ref in enumerate(part_refs):
        block = lax.axis_index("cand") ^ bit
        rows_ref[aligned(block, part_ref.shape[0]), :] = part_ref[:, pl.ds(0, width)]
        lanes = part_ref[:, pl.ds(width, LANES)].astype(F32)
        logit_ref[pl.ds(block, 1), :] = jnp.sum(lanes.T, axis=0, keepdims=True)


def split_low(axis_bit, terms_ref, keep_ref, send_ref, size):
    for pair in range(keep_ref.shape[0] // size):
        rows = pl.ds(pair * size, size)
        keep_ref[rows, :] = terms_ref[aligned(2 * pair + axis_bit, size), :]
        send_ref[rows, :] = terms_ref[aligned(2 * pair + 1 - axis_bit, size), :].astype(BF16)


def layer_three(row_block, base_ref, weight_ref, rows_ref, keep_ref, send_ref, terms_ref):
    multiply(rows_ref, weight_ref, terms_ref, base_ref)
    model = lax.axis_index("mp")
    add_own_columns(terms_ref, rows_ref, model, lax.axis_index("cand"))
    split_low(model % 2, terms_ref, keep_ref, send_ref, row_block)


def halve(row_block, bit, keep_ref, other_ref, kept_ref, send_ref, terms_ref):
    terms_ref[...] = keep_ref[...] + other_ref[...].astype(F32)
    split_low((lax.axis_index("mp") // bit) % 2, terms_ref, kept_ref, send_ref, row_block)


def finish(keep_ref, other_ref, base_ref, bias_ref, total_ref, part_ref, out_ref, logit_ref, sum_ref):
    model = lax.axis_index("mp")
    base = base_ref[aligned(model, out_ref.shape[0]), :].astype(F32)
    cross = keep_ref[...] + other_ref[...].astype(F32) + base * bias_ref[...]
    out_ref[...] = cross.astype(BF16)
    sum_ref[...] = total_ref[...] + part_ref[...]
    logit_ref[...] = sum_ref[pl.ds(model, 1), :]


def finish_scored(keep_ref, other_ref, base_ref, bias_ref, score_ref, out_ref, logit_ref):
    base = base_ref[aligned(lax.axis_index("mp"), out_ref.shape[0]), :].astype(F32)
    cross = keep_ref[...] + other_ref[...].astype(F32) + base * bias_ref[...]
    out_ref[...] = cross.astype(BF16)
    logit_ref[...] = jnp.sum(cross * score_ref[...].astype(F32), axis=1, keepdims=True)


def body(
    user_feats,
    user_slot,
    cand_pool,
    cand_ids,
    first_weight,
    first_bias,
    second_weight,
    second_bias,
    third_weight,
    third_bias,
    score_weight,
):
    cand_count = lax.axis_size("cand")
    model_count = lax.axis_size("mp")
    local, half_width = user_feats.shape
    full_width = 2 * half_width
    user_count, per_user = cand_ids.shape
    row_total = user_count * per_user
    col_block = full_width // cand_count
    feat_block = full_width // model_count
    local_rows = row_total // cand_count
    row_block = row_total // model_count
    half_rows = row_total // 2
    flops = 2 * row_total * col_block * feat_block
    direct = cand_count <= DIRECT and cand_count == model_count
    score, bias = score_weight.reshape(1, -1), third_bias.reshape(1, -1)

    if local > 1:
        user_feats = jnp.take(user_feats, user_slot % local, axis=0)
    elif user_count > 1:
        user_feats = jnp.broadcast_to(user_feats, (user_count, half_width))
    (staged,) = call(stage, [((8, 128), F32)], [], flops=STAGE_FLOPS)
    users = user_feats
    pool_model, pool_cand = call(
        functools.partial(choose_pool, half_width),
        [
            ((row_total, feat_block), BF16),
            ((row_total, col_block), BF16),
        ],
        [cand_ids, cand_pool, staged],
        limit=8 * MIB,
    )
    (want,) = call(
        functools.partial(owner_steps, local),
        [((user_count, 128), jnp.int32)],
        [user_slot],
        smem=(0,),
    )
    if direct:
        users = [users] + [swap(users, "cand", bit) for bit in range(1, cand_count)]
    else:
        slots = user_slot.reshape(-1, 1)
        for bit in bits_of(cand_count):
            (users,) = call(
                functools.partial(choose_user, local, bit),
                [((user_count, half_width), BF16)],
                [slots, users, swap(users, "cand", bit)],
            )
        users = [users]

    half_outs = [((half_rows, col_block), F32), ((half_rows, col_block), BF16)]
    keep, send = call(
        functools.partial(pool_terms, half_width),
        half_outs,
        [pool_model, first_weight],
        scratch=[pltpu.VMEM((row_total, col_block), F32)],
        flops=flops,
        limit=12 * MIB,
    )
    base_model, base_cand, user_sum = call(
        functools.partial(user_terms, half_width),
        [
            ((row_total, feat_block), BF16),
            ((row_total, col_block), BF16),
            ((user_count, col_block), F32),
        ],
        [want, first_weight, pool_model, pool_cand, *users],
        flops=flops,
        limit=12 * MIB,
    )
    keep, send = call(merge, half_outs, [keep, send, user_sum])
    *bits, last_bit = bits_of(model_count)
    assert bits
    for bit in [*bits, last_bit]:
        keep, send = call(add_up, half_outs, [keep, swap(send, "mp", bit)])
    pool_other = swap(send, "mp", 1)

    if direct:
        outs = [
            ((local_rows, feat_block + LANES), BF16 if bit else F32) for bit in range(cand_count)
        ]
        maps = call(
            functools.partial(score_map, half_width, user_count),
            outs,
            [base_cand, score, bias, third_weight],
            scratch=[
                pltpu.VMEM((row_total, col_block), BF16),
                pltpu.VMEM((row_total, feat_block), F32),
                pltpu.VMEM((row_total, col_block), F32),
            ],
            flops=flops,
            limit=12 * MIB,
        )
        maps = [maps[0]] + [swap(maps[bit], "cand", bit) for bit in range(1, cand_count)]
        outs = [((local_rows, feat_block), BF16 if bit else F32) for bit in range(cand_count)]
    else:
        outs = [((row_total, feat_block), BF16)]
    parts = call(
        layer_two,
        outs,
        [
            keep, pool_other, first_bias.reshape(1, -1), base_cand, base_model, second_weight,
        ],
        scratch=[
            pltpu.VMEM((row_total, col_block), BF16),
            pltpu.VMEM((row_total, feat_block), F32),
        ],
        flops=flops,
        limit=12 * MIB,
    )
    if direct:
        parts = [parts[0]] + [swap(parts[bit], "cand", bit) for bit in range(1, cand_count)]
    else:
        parts = [lax.psum_scatter(parts[0], "cand", scatter_dimension=0, tiled=True)]
    bias_two = second_bias.reshape(1, -1)
    if direct:
        (block,) = call(
            functools.partial(cross_scored, cand_count),
            [((local_rows, feat_block + LANES), BF16)],
            [base_model, bias_two, *parts, *maps],
        )
        parts = [block] + [swap(block, "cand", bit) for bit in range(1, cand_count)]
        logit_out = [((cand_count, local_rows), F32)]
        cross_two, logits = call(assemble, [((row_total, feat_block), BF16)] + logit_out, parts)
    else:
        (block,) = call(
            cross_rows, [((local_rows, feat_block), BF16)], [base_model, bias_two, *parts]
        )
        cross_two = lax.all_gather(block, "cand", axis=0, tiled=True)
    rows = row_total // 2
    keep, send = call(
        functools.partial(layer_three, row_block),
        [((rows, col_block), F32), ((rows, col_block), BF16)],
        [base_cand, third_weight, cross_two],
        scratch=[pltpu.VMEM((row_total, col_block), F32)],
        flops=flops,
        limit=12 * MIB,
    )
    other = swap(send, "mp", 1)
    for bit in bits_of(model_count)[1:]:
        scratch = [pltpu.VMEM((rows, col_block), F32)]
        rows //= 2
        keep, send = call(
            functools.partial(halve, row_block, bit),
            [((rows, col_block), F32), ((rows, col_block), BF16)],
            [keep, other],
            scratch=scratch,
        )
        other = swap(send, "mp", bit)

    rows = [keep, other, base_cand, bias]
    crossed_out = ((row_block, col_block), BF16)
    if direct:
        for bit in bits:
            (logits,) = call(add_to, logit_out, [logits, swap(logits, "mp", bit)])
        crossed, logits = call(
            finish,
            [crossed_out, ((1, row_block), F32)],
            [*rows, logits, swap(logits, "mp", last_bit)],
            scratch=[pltpu.VMEM((cand_count, local_rows), F32)],
        )
    else:
        crossed, logits = call(finish_scored, [crossed_out, ((row_block, 1), F32)], [*rows, score])
        logits = lax.psum(logits, "cand")
    return (crossed, logits.reshape(-1))


def solution(mesh):
    in_specs = (
        P(("groups", "cand"), None),
        P("groups"),
        P("groups", None),
        P("groups", None),
        P("mp", "cand"),
        P("cand"),
        P("cand", "mp"),
        P("mp"),
        P("mp", "cand"),
        P("cand"),
        P("cand"),
    )
    out_specs = (P(("groups", "mp"), "cand"), P(("groups", "mp")))

    return jax.shard_map(body, mesh=mesh, in_specs=in_specs, out_specs=out_specs, check_vma=False)
```
